32 devices in a mesh: grp: 2 (over x), seq: 8 (over z, y), tp: 2 (over core).
Axes of the slice: x: 2, y: 2, z: 4, core: 2. Of those that a mesh axis runs over, the one named last changes fastest.
Arguments:
- queries: bfloat16 [16384, 1536], P(('grp', 'seq'), 'tp'), parts along dimension 0, may hold values from -6 to 6
- attn_keys: bfloat16 [16384, 1536], P(('grp', 'seq'), 'tp'), parts along dimension 0, may hold values from -6 to 6
- attn_values: bfloat16 [16384, 1536], P(('grp', 'seq'), 'tp'), parts along dimension 0, may hold values from -6 to 6
- out_weight: bfloat16 [1536, 3072], P('tp'), may hold values from -0.15625 to 0.15625
- residual: bfloat16 [16384, 3072], P(('grp', 'seq'), 'tp'), parts along dimension 0, may hold values from -40 to 40
- norm_gain: float32 [3072], P('tp'), may hold values from 0.1 to 1.9
- conv_weight: float32 [31, 3072], P(None, 'tp'), may hold values from -1 to 1
- record_starts: int32 [16], P('grp'), parts along dimension 0, may hold values from 0 to 7039, as said below
- record_lengths: int32 [16], P('grp'), parts along dimension 0, may hold values from 256 to 1153, as said below
Outputs:
- block_out: bfloat16 [16384, 3072], P(('grp', 'seq'), 'tp'), parts along dimension 0
The draws below stay inside these ranges and needn't reach their ends.
There are 2 independent parts, one for each index of `grp`. The reference program is written for one: setup_inputs(seed, part) draws one part's arguments, and reference() takes and returns one part's arrays. A program takes and returns all parts, laid end to end along the dimension named above; an argument that names none is the same for every part. Nothing has to cross between parts.
Inputs may be any that keep to these rules, and one draw needn't show every extreme that they name: `record_starts`: recording r lies in its stretch: frames 0 to 511 for r = 0; frames r * 1024 - 1024 // 2 to (r + 1) * 1024 - 1024 // 2 - 1 for 0 < r < 7; frames (7) * 1024 - 1024 // 2 to 8191 for the last. It starts within the first quarter of its stretch; recording 0 starts at frame 0. `record_lengths`: each recording ends inside its stretch.
All inputs are finite; a program needn't handle non-finite values.
Results may differ from the reference program's by a relative error of at most 0.0025.
Values may be sent and summed in bfloat16 or wider, within the bound.
A program may use at most 128 MiB of HBM per device.

```python
import jax
import jax.numpy as jnp
from jax import lax

D = 3072
HSIZE = 64
WIN = 128
KHALF = 15
REC = 8
TOK_DEV = 1024
HD = 1536
KERNEL = 31
TOKENS = 8192
SLOT = 1024


def query_key_pair(key):
    query_base = jnp.clip(jax.random.normal(jax.random.fold_in(key, 11), (TOKENS, HD), jnp.float32), -4.5, 4.5)
    key_base = jnp.clip(jax.random.normal(jax.random.fold_in(key, 12), (TOKENS, HD), jnp.float32), -4.5, 4.5)
    return (query_base, key_base)


def draw_queries(key, part):
    return query_key_pair(key)[0].astype(jnp.bfloat16)


def draw_attn_keys(key, part):
    return query_key_pair(key)[1].astype(jnp.bfloat16)


def draw_residual(key, part):
    row_scale = jnp.exp(jax.random.uniform(jax.random.fold_in(key, 41), (TOKENS, 1), jnp.float32, jnp.log(0.3), jnp.log(3.0)))
    column_scale = jnp.exp(jax.random.uniform(jax.random.fold_in(key, 42), (1, D), jnp.float32, jnp.log(0.3), jnp.log(3.0)))
    values_base = jnp.clip(jax.random.normal(jax.random.fold_in(key, 45), (TOKENS, D), jnp.float32), -4.0, 4.0)
    return (values_base * row_scale * column_scale).astype(jnp.bfloat16)


def record_layout(key):
    record_index = jnp.arange(REC, dtype=jnp.int32)
    stretch_start = jnp.where(record_index == 0, 0, record_index * SLOT - SLOT // 2)
    stretch_size = jnp.where(record_index == 0, SLOT // 2, jnp.where(record_index == REC - 1, SLOT + SLOT // 2, SLOT))
    quarter = stretch_size // 4
    gap_frames = jax.random.randint(jax.random.fold_in(key, 32), (REC,), 0, quarter)
    gap_frames = jnp.where(record_index == REC - 1, quarter - 1, gap_frames)
    gap_frames = jnp.where((record_index == 0) | (record_index == REC // 2), 0, gap_frames)
    half_size = stretch_size // 2
    span_frames = half_size + jax.random.randint(jax.random.fold_in(key, 33), (REC,), 0, stretch_size - gap_frames - half_size + 1)
    span_frames = jnp.where(record_index == REC // 2, stretch_size, span_frames)
    span_frames = jnp.where(record_index == REC - 1, stretch_size - gap_frames, span_frames)
    span_frames = jnp.where(record_index == 0, SLOT // 4, span_frames)
    return ((stretch_start + gap_frames).astype(jnp.int32), span_frames.astype(jnp.int32))


def draw_record_starts(key, part):
    return record_layout(key)[0]


def draw_record_lengths(key, part):
    return record_layout(key)[1]


def steps_of(own_key, dims, cuts, low, top_value):
    gain, own = 1.0, jax.random.fold_in(own_key, 6)
    for position, shards_of in cuts:
        steps = jnp.exp(jax.random.uniform(jax.random.fold_in(own, position), (shards_of,), jnp.float32, low / len(cuts), top_value / len(cuts)))
        gain = gain * jnp.repeat(steps, dims[position] // shards_of).reshape([-1 if axis == position else 1 for axis in range(len(dims))])
    return gain


def noise(rng, shape, deviation, limit, split=(), kind=jnp.bfloat16):
    array = jax.random.normal(rng, shape, jnp.float32) * deviation
    if len(split) > 0:
        array = steps_of(rng, shape, split, -0.22, 0.18) * array
    return jnp.clip(array, min=-limit, max=limit).astype(kind)


def setup_inputs(seed: int = 0, part: int = 0) -> dict:
    streams_of = jax.random.split(jax.random.key(seed), 10)
    part_splits = jax.random.split(jax.random.fold_in(streams_of[9], part), 10)
    return {
        "queries": draw_queries(jax.random.fold_in(jax.random.fold_in(streams_of[9], part), 71), part),
        "attn_keys": draw_attn_keys(jax.random.fold_in(jax.random.fold_in(streams_of[9], part), 71), part),
        "attn_values": noise(part_splits[2], (TOKENS, HD), 1.0, 6.0, ((0, 8), (1, 2))),
        "out_weight": noise(streams_of[3], (HD, D), HD ** -0.5, 0.15625, ((0, 2),)),
        "residual": draw_residual(jax.random.fold_in(jax.random.fold_in(streams_of[9], part), 71), part),
        "norm_gain": jnp.clip(1.0 + 0.18 * jax.random.normal(streams_of[5], (D,), jnp.float32), 0.1, 1.9),
        "conv_weight": noise(streams_of[6], (KERNEL, D), KERNEL ** -0.5, 1.0, ((1, 2),), jnp.float32),
        "record_starts": draw_record_starts(jax.random.fold_in(jax.random.fold_in(streams_of[9], part), 71), part),
        "record_lengths": draw_record_lengths(jax.random.fold_in(jax.random.fold_in(streams_of[9], part), 71), part),
    }


def segment_of(positions, record_starts, record_lengths):
    inside = (positions[:, None] >= record_starts[None, :]) & (positions[:, None] < (record_starts + record_lengths)[None, :])
    labels = jnp.arange(1, REC + 1, dtype=jnp.int32)
    return (lax.optimization_barrier(jnp.sum(jnp.where(inside, labels[None, :], 0), axis=1)) - 1).astype(jnp.int32)

def attend(query_block, key_block, value_block, query_segment, key_segment):
    block_rows = query_block.shape[0]
    key_span = key_block.shape[0]
    head_count = query_block.shape[1] // HSIZE
    query_heads = query_block.astype(jnp.float32).reshape(block_rows, head_count, HSIZE)
    key_heads = key_block.astype(jnp.float32).reshape(key_span, head_count, HSIZE)
    value_heads = value_block.astype(jnp.float32).reshape(key_span, head_count, HSIZE)
    scores = jnp.einsum('qhd,khd->hqk', query_heads, key_heads) * HSIZE ** (-0.5)
    distance = jnp.arange(key_span)[None, :] - jnp.arange(block_rows)[:, None] - WIN
    allowed = (jnp.abs(distance) <= WIN) & (query_segment[:, None] == key_segment[None, :]) & (query_segment[:, None] >= 0)
    masked = jnp.where(allowed[None], scores, jnp.float32(-1e+30))
    row_max = lax.optimization_barrier(jnp.max(masked, axis=-1, keepdims=True))
    exponent = jnp.where(allowed[None], jnp.exp(masked - row_max), jnp.float32(0.0))
    row_total = lax.optimization_barrier(jnp.sum(exponent, axis=-1))
    divisor = jnp.where(query_segment[None, :] >= 0, row_total, jnp.float32(1.0))
    weights = lax.optimization_barrier(exponent.astype(jnp.bfloat16)).astype(jnp.float32)
    mixed_heads = jnp.einsum('hqk,khd->qhd', weights, value_heads) / jnp.transpose(divisor)[:, :, None]
    mixed_heads = jnp.where(query_segment[:, None, None] >= 0, mixed_heads, jnp.float32(0.0))
    return mixed_heads.reshape(block_rows, head_count * HSIZE).astype(jnp.bfloat16)

def reference(queries, attn_keys, attn_values, out_weight, residual, norm_gain, conv_weight, record_starts, record_lengths):
    frames = queries.shape[0]
    positions = jnp.arange(frames, dtype=jnp.int32)
    segment = segment_of(positions, record_starts, record_lengths)
    valid = segment >= 0
    block_rows = min(256, TOK_DEV)
    padded_keys = jnp.pad(attn_keys, ((WIN, WIN), (0, 0)))
    padded_values = jnp.pad(attn_values, ((WIN, WIN), (0, 0)))
    padded_segment = jnp.pad(segment, (WIN, WIN), constant_values=-1).astype(jnp.int32)

    def one_block(block_id):
        block_start = (block_id * block_rows).astype(jnp.int32)
        query_block = lax.dynamic_slice_in_dim(queries, block_start, block_rows, 0)
        key_block = lax.dynamic_slice_in_dim(padded_keys, block_start, block_rows + 2 * WIN, 0)
        value_block = lax.dynamic_slice_in_dim(padded_values, block_start, block_rows + 2 * WIN, 0)
        query_segment = lax.dynamic_slice_in_dim(segment, block_start, block_rows, 0)
        key_segment = lax.dynamic_slice_in_dim(padded_segment, block_start, block_rows + 2 * WIN, 0)
        return attend(query_block, key_block, value_block, query_segment, key_segment)
    blocks = lax.map(one_block, jnp.arange(frames // block_rows, dtype=jnp.int32))
    attended = blocks.reshape(frames, -1)
    projected = jnp.dot(attended, out_weight, preferred_element_type=jnp.float32)
    hidden_sum = residual.astype(jnp.float32) + projected
    row_mean = lax.optimization_barrier(jnp.mean(hidden_sum, axis=1, keepdims=True))
    centered = hidden_sum - row_mean
    row_var = lax.optimization_barrier(jnp.mean(centered * centered, axis=1, keepdims=True))
    normed = centered * lax.rsqrt(row_var + jnp.float32(1e-05)) * norm_gain[None, :]
    normed = jnp.where(valid[:, None], normed, jnp.float32(0.0)).astype(jnp.bfloat16)
    padded_normed = jnp.pad(normed, ((KHALF, KHALF), (0, 0)))
    normed_segment = jnp.pad(segment, (KHALF, KHALF), constant_values=-1).astype(jnp.int32)
    conv_sum = jnp.zeros(hidden_sum.shape, jnp.float32)
    for tap_index in range(KERNEL):
        shifted = padded_normed[tap_index:tap_index + frames].astype(jnp.float32)
        same_record = normed_segment[tap_index:tap_index + frames] == segment
        conv_sum = conv_sum + jnp.where(same_record[:, None], conv_weight[tap_index][None, :] * shifted, jnp.float32(0.0))
    return (hidden_sum + jax.nn.silu(conv_sum)).astype(jnp.bfloat16)
```

```python
import functools

import jax
import jax.numpy as jnp
from jax import lax
from jax.experimental import pallas as pl
from jax.experimental.pallas import tpu as pltpu
from jax.sharding import PartitionSpec as P

HSIZE = 64
WIN = 128
KHALF = 15
REC = 8
KERNEL = 31
BLOCK = 128
CHUNK = 256
EDGE = 16
PHASES = 4
HALF = 64
COARSE = 16
STEPS = 9
FIX = 64

F32 = jnp.float32
BF16 = jnp.bfloat16
MESH = pl.DeviceIdType.MESH


def label_of(positions, starts, lengths):
    label = jnp.full(positions.shape, -1, jnp.int32)
    for r in range(REC):
        first = starts[r]
        inside = (positions >= first) & (positions < first + lengths[r])
        label = jnp.where(inside, r, label)
    return label


def block_kernel(
    starts, lengths, q_hbm, k_hbm, v_hbm, w_hbm, res_hbm, gain_ref,
    hid_hbm, nrm_hbm,
    qb, kb, vb, wb, att, resb, hidb, nb, bias_ref, stat, peer,
    in_sem, send_sem, recv_sem, att_send, att_recv, stat_send, stat_recv, out_sem,
):
    frames, width = qb.shape
    feats = resb.shape[1]
    blocks, chunks = frames // BLOCK, frames // CHUNK
    seq, seqs = lax.axis_index("seq"), lax.axis_size("seq")
    tp = lax.axis_index("tp")
    other = 1 - tp
    has_left, has_right = seq > 0, seq < seqs - 1
    left, right = {"seq": seq - 1}, {"seq": seq + 1}
    mate = {"tp": other}

    def local(i, src, dst):
        return pltpu.make_async_copy(src, dst, in_sem.at[i])

    def remote(src, dst, i, to):
        return pltpu.make_async_remote_copy(
            src, dst, send_sem.at[i], recv_sem.at[i], device_id=to, device_id_type=MESH
        )

    def columns(owner):
        return pl.ds(pl.multiple_of(owner * feats, 128), feats)

    loads = (
        local(0, k_hbm, kb.at[pl.ds(WIN, frames)]),
        local(1, v_hbm, vb.at[pl.ds(WIN, frames)]),
        local(2, q_hbm, qb),
        local(3, w_hbm.at[:, columns(tp)], wb.at[tp]),
        local(4, res_hbm, resb),
    )
    for load in loads[:3]:
        load.start()

    barrier = pltpu.get_barrier_semaphore()
    pl.semaphore_signal(barrier, inc=1, device_id=mate, device_id_type=MESH)

    @pl.when(has_left)
    def _():
        pl.semaphore_signal(barrier, inc=1, device_id=left, device_id_type=MESH)

    @pl.when(has_right)
    def _():
        pl.semaphore_signal(barrier, inc=1, device_id=right, device_id_type=MESH)

    pl.semaphore_wait(barrier, 1 + jnp.minimum(seq, 1) + jnp.minimum(seqs - 1 - seq, 1))

    tail, head = pl.ds(frames - WIN, WIN), pl.ds(0, WIN)
    low, high = pl.ds(0, WIN), pl.ds(WIN + frames, WIN)
    to_right = (
        remote(k_hbm.at[tail], kb.at[low], 0, right),
        remote(v_hbm.at[tail], vb.at[low], 1, right),
    )
    to_left = (
        remote(k_hbm.at[head], kb.at[high], 2, left),
        remote(v_hbm.at[head], vb.at[high], 3, left),
    )
    to_mate = remote(w_hbm.at[:, columns(other)], wb.at[tp], 4, mate)

    @pl.when(has_right)
    def _():
        for copy in to_right:
            copy.start()

    @pl.when(has_left)
    def _():
        for copy in to_left:
            copy.start()

    to_mate.start()

    @pl.when(jnp.logical_not(has_left))
    def _():
        kb[low] = jnp.zeros((WIN, width), BF16)
        vb[low] = jnp.zeros((WIN, width), BF16)

    @pl.when(jnp.logical_not(has_right))
    def _():
        kb[high] = jnp.zeros((WIN, width), BF16)
        vb[high] = jnp.zeros((WIN, width), BF16)

    for load in loads[:3]:
        load.wait()
    for load in loads[3:]:
        load.start()

    anchor = seq * frames
    span = BLOCK + 2 * WIN
    lane = lax.broadcasted_iota(jnp.int32, (BLOCK, 128), 1)
    front = lane < HSIZE
    ones = jnp.ones((span, 128), BF16)

    def att_copy(b):
        rows = pl.ds(pl.multiple_of(b * BLOCK, BLOCK), BLOCK)
        return pltpu.make_async_remote_copy(
            att.at[tp, rows], att.at[tp, rows], att_send.at[b], att_recv.at[b],
            device_id=mate, device_id_type=MESH,
        )

    def attend(step, carry):
        b = lax.rem(step + 1, blocks)

        @pl.when((step == blocks - 2) & has_left)
        def _():
            for copy in to_right:
                copy.wait_recv()

        @pl.when((step == blocks - 2) & has_right)
        def _():
            for copy in to_left:
                copy.wait_recv()

        row = pl.multiple_of(b * BLOCK, BLOCK)
        rows = pl.ds(row, BLOCK)
        keys = pl.ds(row, span)
        q_pos = lax.broadcasted_iota(jnp.int32, (BLOCK, 1), 0)
        k_pos = lax.broadcasted_iota(jnp.int32, (1, span), 1)
        q_seg = label_of(anchor + row + q_pos, starts, lengths)
        k_seg = label_of(anchor + row - WIN + k_pos, starts, lengths)
        gap = k_pos - q_pos
        allowed = (gap >= 0) & (gap <= 2 * WIN) & (q_seg == k_seg) & (q_seg >= 0)
        bias_ref[...] = jnp.where(allowed, F32(0.0), F32(-1e30))
        valid = q_seg >= 0
        for pair in range(width // 128):
            lanes = pl.ds(pair * 128, 128)
            q = qb[rows, lanes] * BF16(HSIZE**-0.5)
            zero = jnp.zeros_like(q)
            values = jnp.concatenate([vb[keys, lanes], ones], axis=1)
            heads = []
            for own in (jnp.where(front, q, zero), jnp.where(front, zero, q)):
                scores = bias_ref[...] + lax.dot_general(
                    own, kb[keys, lanes], (((1,), (1,)), ((), ())), preferred_element_type=F32
                )
                top = jnp.max(scores, axis=1, keepdims=True)
                weights = jnp.exp(scores - top).astype(BF16)
                mixed = jnp.dot(weights, values, preferred_element_type=F32)
                heads.append(mixed[:, :128] / mixed[:, 128:])
            mixed = jnp.where(front, heads[0], heads[1])
            att[tp, rows, lanes] = jnp.where(valid, mixed, F32(0.0)).astype(BF16)
        att_copy(b).start()
        return carry

    lax.fori_loop(0, blocks - 2, attend, 0)

    loads[3].wait()
    to_mate.wait_recv()
    loads[4].wait()

    def stat_copy(c):
        rows = pl.ds(pl.multiple_of(c * CHUNK, CHUNK), CHUNK)
        return pltpu.make_async_remote_copy(
            stat.at[rows], peer.at[rows], stat_send.at[c], stat_recv.at[c],
            device_id=mate, device_id_type=MESH,
        )

    def hid_copy(c):
        rows = pl.ds(pl.multiple_of(c * CHUNK, CHUNK), CHUNK)
        return pltpu.make_async_copy(hidb.at[rows], hid_hbm.at[rows], out_sem.at[c])

    def nrm_copy(c):
        rows = pl.ds(pl.multiple_of(EDGE + c * CHUNK, EDGE), CHUNK)
        return pltpu.make_async_copy(nb.at[rows], nrm_hbm.at[rows], out_sem.at[chunks + c])

    chunk_lane = lax.broadcasted_iota(jnp.int32, (CHUNK, 128), 1)
    tile = min(512, feats)

    def project(step, carry):
        c = lax.rem(step + 1, chunks)
        for part in range(CHUNK // BLOCK):
            att_copy(c * (CHUNK // BLOCK) + part).wait_recv()
        rows = pl.ds(pl.multiple_of(c * CHUNK, CHUNK), CHUNK)
        total = jnp.zeros((CHUNK, 1), F32)
        for t in range(feats // tile):
            cols = pl.ds(t * tile, tile)
            hidden = resb[rows, cols].astype(F32)
            for part in range(2):
                hidden += jnp.dot(att[part, rows], wb[part, :, cols], preferred_element_type=F32)
            hidb[rows, cols] = hidden
            total += jnp.sum(hidden, axis=1, keepdims=True)
        mean = total * F32(1.0 / feats)
        spread = jnp.zeros((CHUNK, 1), F32)
        for t in range(feats // tile):
            centered = hidb[rows, pl.ds(t * tile, tile)] - mean
            spread += jnp.sum(centered * centered, axis=1, keepdims=True)
        stat[rows] = jnp.where(chunk_lane < 64, mean, spread)
        stat_copy(c).start()
        hid_copy(c).start()
        return carry

    lax.fori_loop(0, chunks - 2, project, 0)

    first_rows, last_rows = pl.ds(EDGE, EDGE), pl.ds(frames, EDGE)
    low_edge, high_edge = pl.ds(0, EDGE), pl.ds(frames + EDGE, EDGE)
    edge_right = remote(nb.at[last_rows], nb.at[low_edge], 5, right)
    edge_left = remote(nb.at[first_rows], nb.at[high_edge], 6, left)

    def normalise(step, carry):
        c = lax.rem(step + chunks - 1, chunks)
        stat_copy(c).wait_recv()
        row = pl.multiple_of(c * CHUNK, CHUNK)
        rows = pl.ds(row, CHUNK)
        mine, theirs = stat[rows], peer[rows]
        mean_a, mean_b = mine[:, 0:1], theirs[:, 0:1]
        spread = mine[:, 64:65] + theirs[:, 64:65]
        shift = mean_a - mean_b
        variance = (spread + shift * shift * F32(feats / 2)) * F32(1.0 / (2 * feats))
        mean = (mean_a + mean_b) * F32(0.5)
        seg = label_of(
            anchor + row + lax.broadcasted_iota(jnp.int32, (CHUNK, 1), 0), starts, lengths
        )
        scale = jnp.where(seg >= 0, lax.rsqrt(variance + F32(1e-05)), F32(0.0))
        for t in range(feats // tile):
            cols = pl.ds(t * tile, tile)
            normed = (hidb[rows, cols] - mean) * scale * gain_ref[cols][None, :]
            nb[pl.ds(pl.multiple_of(row + EDGE, EDGE), CHUNK), cols] = normed.astype(BF16)
        nrm_copy(c).start()

        @pl.when((step == 0) & has_right)
        def _():
            edge_right.start()

        @pl.when((step == 1) & has_left)
        def _():
            edge_left.start()

        return carry

    lax.fori_loop(2, chunks, normalise, 0)
    lax.fori_loop(blocks - 2, blocks, attend, 0)
    lax.fori_loop(chunks - 2, chunks, project, 0)
    lax.fori_loop(0, 2, normalise, 0)

    @pl.when(has_left)
    def _():
        edge_right.wait_recv()

    @pl.when(jnp.logical_not(has_left))
    def _():
        nb[low_edge] = jnp.zeros((EDGE, feats), BF16)

    @pl.when(has_right)
    def _():
        edge_left.wait_recv()

    @pl.when(jnp.logical_not(has_right))
    def _():
        nb[high_edge] = jnp.zeros((EDGE, feats), BF16)

    edges = (
        pltpu.make_async_copy(nb.at[low_edge], nrm_hbm.at[low_edge], out_sem.at[2 * chunks]),
        pltpu.make_async_copy(nb.at[high_edge], nrm_hbm.at[high_edge], out_sem.at[2 * chunks + 1]),
    )
    for copy in edges:
        copy.start()

    @pl.when(has_right)
    def _():
        for copy in (*to_right, edge_right):
            copy.wait_send()

    @pl.when(has_left)
    def _():
        for copy in (*to_left, edge_left):
            copy.wait_send()

    to_mate.wait_send()

    def drain(c, carry):
        stat_copy(c).wait_send()
        hid_copy(c).wait()
        nrm_copy(c).wait()
        for part in range(CHUNK // BLOCK):
            att_copy(c * (CHUNK // BLOCK) + part).wait_send()
        return carry

    lax.fori_loop(0, chunks, drain, 0)
    for copy in edges:
        copy.wait()


def conv_kernel(
    starts, lengths, anchor_ref, hid_ref, nrm_ref, taps_ref, out_ref,
    wide, padded, rows_of, shaped, weights, sums, valid_ref, eye_ref, near, cuts, count,
):
    frames, lanes = hid_ref.shape
    anchor = anchor_ref[0]
    span = frames // COARSE
    units = span // PHASES
    front = lax.broadcasted_iota(jnp.int32, (COARSE, 128), 1) < HALF

    @pl.when(pl.program_id(0) == 0)
    def _():
        place = anchor + lax.broadcasted_iota(jnp.int32, (frames, 128), 0)
        valid_ref[...] = jnp.where(label_of(place, starts, lengths) >= 0, F32(1.0), F32(0.0))
        across = lax.broadcasted_iota(jnp.int32, (HALF, 256), 1) % HALF
        down = lax.broadcasted_iota(jnp.int32, (HALF, 256), 0)
        eye_ref[...] = jnp.where(across == down, F32(1.0), F32(0.0)).astype(BF16)
        padded[...] = jnp.zeros_like(padded)
        found = jnp.int32(0)
        for r in range(1, REC):
            first = starts[r]
            cuts[found] = first - anchor
            close = (starts[r - 1] + lengths[r - 1] + EDGE > first)
            here = (first > anchor - EDGE) & (first < anchor + frames + EDGE)
            found = found + jnp.where(close & here, 1, 0)
        count[0] = found

    pitch = span + 1
    for r in range(-(-(frames + 2 * EDGE) // span)):
        size = min(span, frames + 2 * EDGE - r * span)
        wide[r * pitch : r * pitch + size, :] = nrm_ref[r * span : r * span + size, :].astype(F32)
    padded[8 : 8 + KERNEL, :] = taps_ref[...]

    def half_pairs(a, b):
        keep = lax.broadcasted_iota(jnp.int32, a.shape, 1) < HALF
        return jnp.where(keep, a, pltpu.roll(b, HALF, 1)), jnp.where(keep, pltpu.roll(a, HALF, 1), b)

    for u in range(units + STEPS - 1):
        at = [wide[pl.ds(PHASES * u + f + (PHASES * u + f) // span, COARSE, stride=pitch), :] for f in range(PHASES)]
        low_a, high_a = half_pairs(at[0], at[1])
        low_b, high_b = half_pairs(at[2], at[3])
        rows = pl.ds(u * COARSE, COARSE)
        shaped[0, rows, 0:128] = low_a.astype(BF16)
        shaped[0, rows, 128:256] = low_b.astype(BF16)
        shaped[1, rows, 0:128] = high_a.astype(BF16)
        shaped[1, rows, 128:256] = high_b.astype(BF16)

    shifted = [padded[7 - p : 47 - p, :] for p in range(PHASES)]
    low_a, high_a = half_pairs(shifted[0], shifted[1])
    low_b, high_b = half_pairs(shifted[2], shifted[3])
    rows_of[0, :, 0:128] = low_a
    rows_of[0, :, 128:256] = low_b
    rows_of[1, :, 0:128] = high_a
    rows_of[1, :, 128:256] = high_b
    results = []
    for h in range(2):
        for v in range(PHASES * STEPS):
            row = jnp.broadcast_to(rows_of[h, v : v + 1, :], (16, 256)).astype(BF16)
            for part in range(HALF // 16):
                weights[h, pl.ds(v * HALF + part * 16, 16), :] = row * eye_ref[pl.ds(part * 16, 16), :]
        left = jnp.concatenate(
            [shaped[h, pl.ds(s * COARSE, units * COARSE), :] for s in range(STEPS)], axis=1
        )
        results.append(jnp.dot(left, weights[h], preferred_element_type=F32))
    pair = half_pairs(results[0][:, :128], results[1][:, :128]) + half_pairs(
        results[0][:, 128:], results[1][:, 128:]
    )
    for p in range(PHASES):
        for u in range(units):
            sums[pl.ds(PHASES * u + p, COARSE, stride=pitch), :] = pair[p][u * COARSE : (u + 1) * COARSE]

    def finish(total, valid, hidden):
        total = total * valid
        return (hidden + silu(total)).astype(BF16)

    for r in range(COARSE):
        rows = pl.ds(r * span, span)
        out_ref[rows, :] = finish(sums[r * pitch : r * pitch + span, :], valid_ref[rows, :], hid_ref[rows, :])

    def fix(i, carry):
        cut = cuts[i]
        base = pl.multiple_of(jnp.clip((cut - EDGE) // 16 * 16, 0, frames - FIX), 16)
        near[...] = nrm_ref[pl.ds(base, FIX + 2 * EDGE), :].astype(F32)
        octets = base + 8 * lax.broadcasted_iota(jnp.int32, (FIX // 8, 128), 0)
        zero = jnp.zeros((FIX // 8, 128), F32)
        before = [zero] * 8
        after = [zero] * 8
        for offset in range(1, KERNEL + 8):
            window = near[pl.ds(offset, FIX // 8, stride=8), :]
            late = octets + (offset - EDGE) >= cut
            window_after = jnp.where(late, window, zero)
            window_before = jnp.where(late, zero, window)
            for phase in range(8):
                tap = offset - 1 - phase
                if 0 <= tap < KERNEL:
                    weight = jnp.broadcast_to(taps_ref[tap : tap + 1, :], (FIX // 8, 128))
                    before[phase] += weight * window_before
                    after[phase] += weight * window_after
        for phase in range(8):
            late = octets + phase >= cut
            near[pl.ds(phase, FIX // 8, stride=8), :] = jnp.where(late, after[phase], before[phase])
        rows = pl.ds(base, FIX)
        out_ref[rows, :] = finish(near[0:FIX, :], valid_ref[rows, :], hid_ref[rows, :])
        return carry

    lax.fori_loop(0, count[0], fix, 0)


def silu(total):
    return total * (F32(0.5) + F32(0.5) * jnp.tanh(total * F32(0.5)))


def conv(starts, lengths, anchor, hidden, normed, taps):
    frames, feats = hidden.shape
    scalars = pl.BlockSpec(memory_space=pltpu.SMEM)
    LANES = 128
    tall = (frames // (COARSE * PHASES) + STEPS - 1) * COARSE
    return pl.pallas_call(
        conv_kernel,
        out_shape=jax.ShapeDtypeStruct((frames, feats), BF16),
        grid=(feats // LANES,),
        in_specs=[scalars, scalars, scalars]
        + [
            pl.BlockSpec((frames, LANES), lambda j: (0, j)),
            pl.BlockSpec((frames + 2 * EDGE, LANES), lambda j: (0, j)),
            pl.BlockSpec((KERNEL, LANES), lambda j: (0, j)),
        ],
        out_specs=pl.BlockSpec((frames, LANES), lambda j: (0, j)),
        scratch_shapes=[
            pltpu.VMEM((frames + 2 * EDGE + 24, 128), F32),
            pltpu.VMEM((48, 128), F32),
            pltpu.VMEM((2, 40, 256), F32),
            pltpu.VMEM((2, tall, 256), BF16),
            pltpu.VMEM((2, PHASES * STEPS * HALF, 256), BF16),
            pltpu.VMEM((frames + COARSE, 128), F32),
            pltpu.VMEM((frames, 128), F32),
            pltpu.VMEM((HALF, 256), BF16),
            pltpu.VMEM((FIX + 2 * EDGE, 128), F32),
            pltpu.SMEM((REC,), jnp.int32),
            pltpu.SMEM((1,), jnp.int32),
        ],
        compiler_params=pltpu.CompilerParams(vmem_limit_bytes=40 * 2**20),
        name="conv",
    )(starts, lengths, anchor, hidden, normed, taps)


def on_device(q, k, v, weight, residual, gain, taps, starts, lengths):
    frames, width = q.shape
    feats = residual.shape[1]
    chunks, blocks = frames // CHUNK, frames // BLOCK
    anywhere = pl.BlockSpec(memory_space=pl.ANY)
    scalars = pl.BlockSpec(memory_space=pltpu.SMEM)
    dma = pltpu.SemaphoreType.DMA
    hidden, normed = pl.pallas_call(
        block_kernel,
        out_shape=(
            jax.ShapeDtypeStruct((frames, feats), F32),
            jax.ShapeDtypeStruct((frames + 2 * EDGE, feats), BF16),
        ),
        in_specs=[scalars, scalars] + [anywhere] * 5 + [pl.BlockSpec(memory_space=pltpu.VMEM)],
        out_specs=(anywhere, anywhere),
        scratch_shapes=[
            pltpu.VMEM((frames, width), BF16),
            pltpu.VMEM((frames + 2 * WIN, width), BF16),
            pltpu.VMEM((frames + 2 * WIN, width), BF16),
            pltpu.VMEM((2, width, feats), BF16),
            pltpu.VMEM((2, frames, width), BF16),
            pltpu.VMEM((frames, feats), BF16),
            pltpu.VMEM((frames, feats), F32),
            pltpu.VMEM((frames + 2 * EDGE, feats), BF16),
            pltpu.VMEM((BLOCK, BLOCK + 2 * WIN), F32),
            pltpu.VMEM((frames, 128), F32),
            pltpu.VMEM((frames, 128), F32),
            dma((5,)), dma((7,)), dma((7,)), dma((blocks,)), dma((blocks,)),
            dma((chunks,)), dma((chunks,)), dma((2 * chunks + 2,)),
        ],
        compiler_params=pltpu.CompilerParams(
            collective_id=0, has_side_effects=True, vmem_limit_bytes=56 * 2**20
        ),
        name="mix",
    )(starts, lengths, q, k, v, weight, residual, gain)
    anchor = (lax.axis_index("seq") * frames).astype(jnp.int32).reshape(1)
    return conv(starts, lengths, anchor, hidden, normed, taps)


def solution(mesh):
    placed = (
        P(("grp", "seq"), "tp"),
        P(("grp", "seq"), "tp"),
        P(("grp", "seq"), "tp"),
        P("tp", None),
        P(("grp", "seq"), "tp"),
        P("tp"),
        P(None, "tp"),
        P("grp"),
        P("grp"),
    )
    return jax.shard_map(
        on_device, mesh=mesh, in_specs=placed, out_specs=P(("grp", "seq"), "tp"), check_vma=False
    )
```

```python
import functools

import jax
import jax.numpy as jnp
from jax import lax
from jax.experimental import pallas as pl
from jax.experimental.pallas import tpu as pltpu
from jax.sharding import PartitionSpec as P

HSIZE = 64
WIN = 128
KHALF = 15
REC = 8
KERNEL = 31
BLOCK = 128
CHUNK = 256
EDGE = 16
PHASES = 4
HALF = 64
COARSE = 16
STEPS = 9
FIX = 64
LANES = 256
EARLY, EARLY_SPAN, LATE_SPAN = 48, 40, 24
FILL = (3, 1, 1, 1)

F32 = jnp.float32
BF16 = jnp.bfloat16
MESH = pl.DeviceIdType.MESH


def label_of(positions, starts, lengths):
    label = jnp.full(positions.shape, -1, jnp.int32)
    for r in range(REC):
        first = starts[r]
        inside = (positions >= first) & (positions < first + lengths[r])
        label = jnp.where(inside, r, label)
    return label


def silu(total):
    return total * (F32(0.5) + F32(0.5) * jnp.tanh(total * F32(0.5)))


def half_pairs(a, b):
    keep = lax.broadcasted_iota(jnp.int32, a.shape, 1) < HALF
    return jnp.where(keep, a, pltpu.roll(b, HALF, 1)), jnp.where(keep, pltpu.roll(a, HALF, 1), b)


def convolve(g, spots, span, wide, padded, rows_of, shaped, weights, sums, eye_ref, nb, taps_ref, emit):
    units = span // PHASES
    reach = span + 2 * EDGE
    pitch, step = reach + 1, span + 1
    cols = pl.ds(pl.multiple_of(g * 128, 128), 128)
    for r, spot in enumerate(spots):
        low = spot // 16 * 16
        high = -(-(spot + reach) // 16) * 16
        block = nb[low:high, cols].astype(F32)
        wide[r * pitch : r * pitch + reach, :] = block[spot - low : spot - low + reach]
    for u in range(units + STEPS - 1):
        at = [wide[pl.ds(PHASES * u + f, COARSE, stride=pitch), :] for f in range(PHASES)]
        low_a, high_a = half_pairs(at[0], at[1])
        low_b, high_b = half_pairs(at[2], at[3])
        rows = pl.ds(u * COARSE, COARSE)
        shaped[0, rows, 0:128] = low_a.astype(BF16)
        shaped[0, rows, 128:256] = low_b.astype(BF16)
        shaped[1, rows, 0:128] = high_a.astype(BF16)
        shaped[1, rows, 128:256] = high_b.astype(BF16)
    padded[8 : 8 + KERNEL, :] = taps_ref[:, cols]
    shifted = [padded[7 - p : 47 - p, :] for p in range(PHASES)]
    low_a, high_a = half_pairs(shifted[0], shifted[1])
    low_b, high_b = half_pairs(shifted[2], shifted[3])
    rows_of[0, :, 0:128] = low_a
    rows_of[0, :, 128:256] = low_b
    rows_of[1, :, 0:128] = high_a
    rows_of[1, :, 128:256] = high_b
    results = []
    for h in range(2):
        for v in range(PHASES * STEPS):
            row = jnp.broadcast_to(rows_of[h, v : v + 1, :], (16, 256)).astype(BF16)
            for part in range(HALF // 16):
                weights[h, pl.ds(v * HALF + part * 16, 16), :] = row * eye_ref[pl.ds(part * 16, 16), :]
        left = jnp.concatenate(
            [shaped[h, pl.ds(s * COARSE, units * COARSE), :] for s in range(STEPS)], axis=1
        )
        results.append(jnp.dot(left, weights[h], preferred_element_type=F32))
    pair = half_pairs(results[0][:, :128], results[1][:, :128]) + half_pairs(
        results[0][:, 128:], results[1][:, 128:]
    )
    for p in range(PHASES):
        for u in range(units):
            sums[pl.ds(PHASES * u + p, COARSE, stride=step), :] = pair[p][u * COARSE : (u + 1) * COARSE]
    for r in range(0, len(spots), 2):
        parts = [sums[(r + i) * step : (r + i) * step + span, :] for i in range(2)]
        emit(spots[r], cols, jnp.concatenate(parts, axis=0))


def fix_kernel(
    starts, lengths, anchor_ref, pre_hbm, hid_hbm, nrm_hbm, taps_hbm, out_hbm,
    held, hidw, nrmw, outw, taps_ref, near, sems,
):
    frames, feats = pre_hbm.shape
    anchor = anchor_ref[0]
    pieces = sems.shape[0]
    whole = []
    for i in range(pieces):
        rows = pl.ds(i * (frames // pieces), frames // pieces)
        whole.append((
            pltpu.make_async_copy(pre_hbm.at[rows], held.at[rows], sems.at[i]),
            pltpu.make_async_copy(held.at[rows], out_hbm.at[rows], sems.at[i]),
        ))
        whole[-1][0].start()
    for fetch, store in whole:
        fetch.wait()
        store.start()
    for fetch, store in whole:
        store.wait()

    def look(r, carry):
        first = starts[r]
        close = starts[r - 1] + lengths[r - 1] + EDGE > first
        here = (first > anchor - EDGE) & (first < anchor + frames + EDGE)

        @pl.when(close & here)
        def _():
            cut = first - anchor
            base = pl.multiple_of(jnp.clip((cut - EDGE) // 16 * 16, 0, frames - FIX), 16)
            rows = pl.ds(base, FIX)
            fetch = (
                pltpu.make_async_copy(hid_hbm.at[rows], hidw, sems.at[0]),
                pltpu.make_async_copy(nrm_hbm.at[pl.ds(base, FIX + 2 * EDGE)], nrmw, sems.at[1]),
                pltpu.make_async_copy(taps_hbm, taps_ref, sems.at[2]),
            )
            for copy in fetch:
                copy.start()
            for copy in fetch:
                copy.wait()
            octets = base + 8 * lax.broadcasted_iota(jnp.int32, (FIX // 8, 128), 0)
            place = anchor + base + lax.broadcasted_iota(jnp.int32, (FIX, 1), 0)
            valid = label_of(place, starts, lengths) >= 0
            zero = jnp.zeros((FIX // 8, 128), F32)

            def column(g, inner):
                cols = pl.ds(pl.multiple_of(g * 128, 128), 128)
                near[...] = nrmw[:, cols].astype(F32)
                before = [zero] * 8
                after = [zero] * 8
                for offset in range(1, KERNEL + 8):
                    window = near[pl.ds(offset, FIX // 8, stride=8), :]
                    late = octets + (offset - EDGE) >= cut
                    window_after = jnp.where(late, window, zero)
                    window_before = jnp.where(late, zero, window)
                    for phase in range(8):
                        tap = offset - 1 - phase
                        if 0 <= tap < KERNEL:
                            weight = jnp.broadcast_to(taps_ref[tap : tap + 1, cols], (FIX // 8, 128))
                            before[phase] += weight * window_before
                            after[phase] += weight * window_after
                for phase in range(8):
                    late = octets + phase >= cut
                    near[pl.ds(phase, FIX // 8, stride=8), :] = jnp.where(late, after[phase], before[phase])
                total = jnp.where(valid, near[0:FIX, :], F32(0.0))
                outw[:, cols] = (hidw[:, cols] + silu(total)).astype(BF16)
                return inner

            lax.fori_loop(0, feats // 128, column, 0)
            done = pltpu.make_async_copy(outw, out_hbm.at[rows], sems.at[0])
            done.start()
            done.wait()

        return carry

    lax.fori_loop(1, REC, look, 0)


def block_kernel(
    starts, lengths, q_hbm, k_hbm, v_hbm, w_hbm, res_hbm, gain_ref, taps_ref,
    pre_hbm, hid_hbm, nrm_hbm,
    qb, kb, kt, vb, wb, att, resb, hidb, nb, stat, peer,
    valid_ref, eye_ref, wide, padded, rows_of, shaped, taps_wide, sums,
    in_sem, send_sem, recv_sem, att_send, att_recv, stat_send, stat_recv, out_sem, pre_sem,
):
    frames, width = qb.shape
    feats = resb.shape[1]
    blocks, chunks = frames // BLOCK, frames // CHUNK
    seq, seqs = lax.axis_index("seq"), lax.axis_size("seq")
    tp = lax.axis_index("tp")
    other = 1 - tp
    has_left, has_right = seq > 0, seq < seqs - 1
    left, right = {"seq": seq - 1}, {"seq": seq + 1}
    mate = {"tp": other}

    def local(i, src, dst):
        return pltpu.make_async_copy(src, dst, in_sem.at[i])

    def remote(src, dst, i, to):
        return pltpu.make_async_remote_copy(
            src, dst, send_sem.at[i], recv_sem.at[i], device_id=to, device_id_type=MESH
        )

    def columns(owner):
        return pl.ds(pl.multiple_of(owner * feats, 128), feats)

    loads = (
        local(0, k_hbm, kb.at[pl.ds(WIN, frames)]),
        local(1, v_hbm, vb.at[pl.ds(WIN, frames)]),
        local(2, q_hbm, qb),
        local(3, w_hbm.at[:, columns(tp)], wb.at[tp]),
        local(4, res_hbm, resb),
    )
    for load in loads[:3]:
        load.start()

    barrier = pltpu.get_barrier_semaphore()
    pl.semaphore_signal(barrier, inc=1, device_id=mate, device_id_type=MESH)

    @pl.when(has_left)
    def _():
        pl.semaphore_signal(barrier, inc=1, device_id=left, device_id_type=MESH)

    @pl.when(has_right)
    def _():
        pl.semaphore_signal(barrier, inc=1, device_id=right, device_id_type=MESH)

    pl.semaphore_wait(barrier, 1 + jnp.minimum(seq, 1) + jnp.minimum(seqs - 1 - seq, 1))

    tail, head = pl.ds(frames - WIN, WIN), pl.ds(0, WIN)
    low, high = pl.ds(0, WIN), pl.ds(WIN + frames, WIN)
    to_right = (
        remote(k_hbm.at[tail], kb.at[low], 0, right),
        remote(v_hbm.at[tail], vb.at[low], 1, right),
    )
    to_left = (
        remote(k_hbm.at[head], kb.at[high], 2, left),
        remote(v_hbm.at[head], vb.at[high], 3, left),
    )
    to_mate = remote(w_hbm.at[:, columns(other)], wb.at[tp], 4, mate)

    @pl.when(has_right)
    def _():
        for copy in to_right:
            copy.start()

    to_mate.start()

    @pl.when(jnp.logical_not(has_left))
    def _():
        kt[:, low] = jnp.zeros((width, WIN), BF16)
        vb[low] = jnp.zeros((WIN, width), BF16)

    @pl.when(jnp.logical_not(has_right))
    def _():
        kt[:, high] = jnp.zeros((width, WIN), BF16)
        vb[high] = jnp.zeros((WIN, width), BF16)

    def turn(i, carry):
        part = pl.ds(pl.multiple_of(i * 128, 128), 128)
        for pair in range(width // 128):
            lanes = pl.ds(pair * 128, 128)
            kt[lanes, part] = jnp.transpose(kb[part, lanes])
        return carry

    anchor = seq * frames
    place = anchor + lax.broadcasted_iota(jnp.int32, (frames, 128), 0)
    inside = place < 0
    for r in range(REC):
        inside |= (place >= starts[r]) & (place < starts[r] + lengths[r])
    valid_ref[...] = jnp.where(inside, F32(1.0), F32(0.0))
    fold = lax.broadcasted_iota(jnp.int32, (HALF, 256), 1) % HALF
    down = lax.broadcasted_iota(jnp.int32, (HALF, 256), 0)
    eye_ref[...] = jnp.where(fold == down, F32(1.0), F32(0.0)).astype(BF16)
    padded[...] = jnp.zeros_like(padded)

    loads[0].wait()
    lax.fori_loop(1, 1 + frames // 128, turn, 0)
    for load in loads[1:3]:
        load.wait()
    for load in loads[3:]:
        load.start()

    span = BLOCK + 2 * WIN

    def att_copy(b):
        rows = pl.ds(pl.multiple_of(b * BLOCK, BLOCK), BLOCK)
        return pltpu.make_async_remote_copy(
            att.at[tp, rows], att.at[tp, rows], att_send.at[b], att_recv.at[b],
            device_id=mate, device_id_type=MESH,
        )

    def attend(b):
        row = pl.multiple_of(b * BLOCK, BLOCK)
        rows = pl.ds(row, BLOCK)
        keys = pl.ds(row, span)
        q_pos = lax.broadcasted_iota(jnp.int32, (BLOCK, 1), 0)
        k_pos = lax.broadcasted_iota(jnp.int32, (1, span), 1)
        q_seg = label_of(anchor + row + q_pos, starts, lengths)
        k_seg = label_of(anchor + row - WIN + k_pos, starts, lengths)
        gap = k_pos - q_pos
        allowed = (gap >= 0) & (gap <= 2 * WIN) & (q_seg == k_seg) & (q_seg >= 0)
        bias = jnp.where(allowed, F32(0.0), F32(-1e30)).astype(BF16)
        valid = q_seg >= 0
        down = lax.broadcasted_iota(jnp.int32, (BLOCK, BLOCK), 0)
        across = lax.broadcasted_iota(jnp.int32, (BLOCK, BLOCK), 1)
        eye = jnp.where(down == across, F32(1.0), F32(0.0)).astype(BF16)
        first = lax.broadcasted_iota(jnp.int32, (span, 128), 1) < HSIZE
        ones = (
            jnp.where(first, F32(1.0), F32(0.0)).astype(BF16),
            jnp.where(first, F32(0.0), F32(1.0)).astype(BF16),
        )
        gap_rows = jnp.zeros((HSIZE, span), BF16)
        for pair in range(width // 128):
            lanes = pl.ds(pair * 128, 128)
            left_side = jnp.concatenate([qb[rows, lanes] * BF16(HSIZE**-0.5), eye], axis=1)
            turned = kt[lanes, keys]
            right_side = jnp.concatenate(
                [
                    jnp.concatenate([turned[:HSIZE], gap_rows, bias], axis=0),
                    jnp.concatenate([gap_rows, turned[HSIZE:], bias], axis=0),
                ],
                axis=1,
            )
            scores = jnp.dot(left_side, right_side, preferred_element_type=F32)
            weights = []
            for own in (scores[:, :span], scores[:, span:]):
                weights.append(jnp.exp(own - jnp.max(own, axis=1, keepdims=True)).astype(BF16))
            v = vb[keys, lanes]
            zero = jnp.zeros_like(v)
            values = jnp.concatenate(
                [
                    jnp.concatenate([jnp.where(first, v, zero), ones[0]], axis=1),
                    jnp.concatenate([jnp.where(first, zero, v), ones[1]], axis=1),
                ],
                axis=0,
            )
            mixed = jnp.dot(jnp.concatenate(weights, axis=1), values, preferred_element_type=F32)
            mixed = mixed[:, :128] / mixed[:, 128:]
            att[tp, rows, lanes] = jnp.where(valid, mixed, F32(0.0)).astype(BF16)
        att_copy(b).start()

    def inner(b, carry):
        attend(b)

        return carry

    lax.fori_loop(1, blocks - 1, inner, 0)

    loads[3].wait()
    to_mate.wait_recv()
    loads[4].wait()

    def stat_copy(c):
        rows = pl.ds(pl.multiple_of(c * CHUNK, CHUNK), CHUNK)
        return pltpu.make_async_remote_copy(
            stat.at[rows], peer.at[rows], stat_send.at[c], stat_recv.at[c],
            device_id=mate, device_id_type=MESH,
        )

    def hid_copy(c):
        rows = pl.ds(pl.multiple_of(c * CHUNK, CHUNK), CHUNK)
        return pltpu.make_async_copy(hidb.at[rows], hid_hbm.at[rows], out_sem.at[c])

    def nrm_copy(c):
        rows = pl.ds(pl.multiple_of(EDGE + c * CHUNK, EDGE), CHUNK)
        return pltpu.make_async_copy(nb.at[rows], nrm_hbm.at[rows], out_sem.at[chunks + c])

    chunk_lane = lax.broadcasted_iota(jnp.int32, (CHUNK, 128), 1)
    tile = min(512, feats)

    def project(c):
        for part in range(CHUNK // BLOCK):
            att_copy(c * (CHUNK // BLOCK) + part).wait_recv()
        rows = pl.ds(pl.multiple_of(c * CHUNK, CHUNK), CHUNK)
        total = jnp.zeros((CHUNK, 1), F32)
        for t in range(feats // tile):
            cols = pl.ds(t * tile, tile)
            hidden = resb[rows, cols].astype(F32)
            for part in range(2):
                hidden += jnp.dot(att[part, rows], wb[part, :, cols], preferred_element_type=F32)
            hidb[rows, cols] = hidden
            total += jnp.sum(hidden, axis=1, keepdims=True)
        mean = total * F32(1.0 / feats)
        spread = jnp.zeros((CHUNK, 1), F32)
        for t in range(feats // tile):
            centered = hidb[rows, pl.ds(t * tile, tile)] - mean
            spread += jnp.sum(centered * centered, axis=1, keepdims=True)
        stat[rows] = jnp.where(chunk_lane < 64, mean, spread)
        stat_copy(c).start()
        hid_copy(c).start()

    first_rows, last_rows = pl.ds(EDGE, EDGE), pl.ds(frames, EDGE)
    low_edge, high_edge = pl.ds(0, EDGE), pl.ds(frames + EDGE, EDGE)
    edge_right = remote(nb.at[last_rows], nb.at[low_edge], 5, right)
    edge_left = remote(nb.at[first_rows], nb.at[high_edge], 6, left)

    def normalise(c):
        stat_copy(c).wait_recv()
        row = pl.multiple_of(c * CHUNK, CHUNK)
        rows = pl.ds(row, CHUNK)
        mine, theirs = stat[rows], peer[rows]
        mean_a, mean_b = mine[:, 0:1], theirs[:, 0:1]
        spread = mine[:, 64:65] + theirs[:, 64:65]
        shift = mean_a - mean_b
        variance = (spread + shift * shift * F32(feats / 2)) * F32(1.0 / (2 * feats))
        mean = (mean_a + mean_b) * F32(0.5)
        scale = lax.rsqrt(variance + F32(1e-05)) * valid_ref[rows, 0:1]
        for t in range(feats // tile):
            cols = pl.ds(t * tile, tile)
            normed = (hidb[rows, cols] - mean) * scale * gain_ref[cols][None, :]
            nb[pl.ds(pl.multiple_of(row + EDGE, EDGE), CHUNK), cols] = normed.astype(BF16)
        nrm_copy(c).start()

    project(jnp.int32(1))

    @pl.when(has_right)
    def _():
        for copy in to_right:
            copy.wait_send()

    @pl.when(has_left)
    def _():
        for copy in to_left:
            copy.start()

    project(jnp.int32(2))
    normalise(jnp.int32(1))

    @pl.when(has_left)
    def _():
        for copy in to_right:
            copy.wait_recv()
        turn(0, 0)

    attend(jnp.int32(0))
    normalise(jnp.int32(2))
    project(jnp.int32(0))
    normalise(jnp.int32(0))

    @pl.when(has_left)
    def _():
        edge_left.start()

    tail_rows = frames - EARLY - COARSE * EARLY_SPAN
    early = [EARLY + EARLY_SPAN * r for r in range(COARSE)]
    late = [EARLY + COARSE * EARLY_SPAN + LATE_SPAN * r for r in range(tail_rows // LATE_SPAN)]
    late += [LATE_SPAN * r for r in range(EARLY // LATE_SPAN)]

    def emit(spot, cols, total):
        rows = pl.ds(spot, total.shape[0])
        resb[rows, cols] = (hidb[rows, cols] + silu(total * valid_ref[rows, :])).astype(BF16)

    def both(spots, size):
        def run(i, carry):
            for half in range(2):
                convolve(
                    i * 2 + half, spots, size, wide.at[half], padded.at[half], rows_of.at[half], shaped.at[half],
                    taps_wide.at[half], sums.at[half], eye_ref, nb, taps_ref, emit,
                )
            return carry

        return run

    early_step, late_step = both(early, EARLY_SPAN), both(late, LATE_SPAN)
    stops = [sum(FILL[:i]) for i in range(len(FILL) + 1)]

    def fill(i):
        lax.fori_loop(stops[i], stops[i + 1], early_step, 0)

    fill(0)

    @pl.when(has_right)
    def _():
        for copy in to_left:
            copy.wait_recv()
        turn(1 + frames // 128, 0)

    attend(jnp.int32(blocks - 1))
    fill(1)
    project(jnp.int32(chunks - 1))
    fill(2)
    normalise(jnp.int32(chunks - 1))

    @pl.when(has_right)
    def _():
        edge_right.start()

    fill(3)

    @pl.when(has_left)
    def _():
        edge_right.wait_recv()

    @pl.when(jnp.logical_not(has_left))
    def _():
        nb[low_edge] = jnp.zeros((EDGE, feats), BF16)

    @pl.when(has_right)
    def _():
        edge_left.wait_recv()

    @pl.when(jnp.logical_not(has_right))
    def _():
        nb[high_edge] = jnp.zeros((EDGE, feats), BF16)

    edges = (
        pltpu.make_async_copy(nb.at[low_edge], nrm_hbm.at[low_edge], out_sem.at[2 * chunks]),
        pltpu.make_async_copy(nb.at[high_edge], nrm_hbm.at[high_edge], out_sem.at[2 * chunks + 1]),
    )
    for copy in edges:
        copy.start()

    def pre_copy(i):
        cols = pl.ds(pl.multiple_of(i * LANES, LANES), LANES)
        return pltpu.make_async_copy(resb.at[:, cols], pre_hbm.at[:, cols], pre_sem.at[i])

    def finish(i, carry):
        late_step(i, 0)
        pre_copy(i).start()
        return carry

    lax.fori_loop(0, feats // LANES, finish, 0)

    @pl.when(has_right)
    def _():
        edge_right.wait_send()

    @pl.when(has_left)
    def _():
        for copy in (*to_left, edge_left):
            copy.wait_send()

    to_mate.wait_send()

    def drain(c, carry):
        stat_copy(c).wait_send()
        hid_copy(c).wait()
        nrm_copy(c).wait()
        for part in range(CHUNK // BLOCK):
            att_copy(c * (CHUNK // BLOCK) + part).wait_send()
        return carry

    lax.fori_loop(0, chunks, drain, 0)

    def leave(i, carry):
        pre_copy(i).wait()
        return carry

    lax.fori_loop(0, feats // LANES, leave, 0)
    for copy in edges:
        copy.wait()


def on_device(q, k, v, weight, residual, gain, taps, starts, lengths):
    frames, width = q.shape
    feats = residual.shape[1]
    chunks, blocks = frames // CHUNK, frames // BLOCK
    anywhere = pl.BlockSpec(memory_space=pl.ANY)
    scalars = pl.BlockSpec(memory_space=pltpu.SMEM)
    dma = pltpu.SemaphoreType.DMA
    tall = (max(EARLY_SPAN, LATE_SPAN) // PHASES + STEPS - 1) * COARSE
    pre, hidden, normed = pl.pallas_call(
        block_kernel,
        out_shape=(
            jax.ShapeDtypeStruct((frames, feats), BF16),
            jax.ShapeDtypeStruct((frames, feats), F32),
            jax.ShapeDtypeStruct((frames + 2 * EDGE, feats), BF16),
        ),
        in_specs=[scalars, scalars] + [anywhere] * 5 + [pl.BlockSpec(memory_space=pltpu.VMEM)] * 2,
        out_specs=(anywhere,) * 3,
        scratch_shapes=[
            pltpu.VMEM((frames, width), BF16),
            pltpu.VMEM((frames + 2 * WIN, width), BF16),
            pltpu.VMEM((width, frames + 2 * WIN), BF16),
            pltpu.VMEM((frames + 2 * WIN, width), BF16),
            pltpu.VMEM((2, width, feats), BF16),
            pltpu.VMEM((2, frames, width), BF16),
            pltpu.VMEM((frames, feats), BF16),
            pltpu.VMEM((frames, feats), F32),
            pltpu.VMEM((frames + 2 * EDGE, feats), BF16),
            pltpu.VMEM((frames, 128), F32),
            pltpu.VMEM((frames, 128), F32),
            pltpu.VMEM((frames, 128), F32),
            pltpu.VMEM((HALF, 256), BF16),
            pltpu.VMEM((2, COARSE * (EARLY_SPAN + 2 * EDGE + 1), 128), F32),
            pltpu.VMEM((2, 48, 128), F32),
            pltpu.VMEM((2, 2, 40, 256), F32),
            pltpu.VMEM((2, 2, tall, 256), BF16),
            pltpu.VMEM((2, 2, PHASES * STEPS * HALF, 256), BF16),
            pltpu.VMEM((2, COARSE * (EARLY_SPAN + 1), 128), F32),
            dma((5,)), dma((7,)), dma((7,)), dma((blocks,)), dma((blocks,)),
            dma((chunks,)), dma((chunks,)), dma((2 * chunks + 2,)), dma((feats // LANES,)),
        ],
        compiler_params=pltpu.CompilerParams(
            collective_id=0, has_side_effects=True, vmem_limit_bytes=60 * 2**20
        ),
        name="mix",
    )(starts, lengths, q, k, v, weight, residual, gain, taps)
    anchor = (lax.axis_index("seq") * frames).astype(jnp.int32).reshape(1)
    return pl.pallas_call(
        fix_kernel,
        out_shape=jax.ShapeDtypeStruct((frames, feats), BF16),
        in_specs=[scalars] * 3 + [anywhere] * 4,
        out_specs=anywhere,
        scratch_shapes=[
            pltpu.VMEM((frames, feats), BF16),
            pltpu.VMEM((FIX, feats), F32),
            pltpu.VMEM((FIX + 2 * EDGE, feats), BF16),
            pltpu.VMEM((FIX, feats), BF16),
            pltpu.VMEM((KERNEL, feats), F32),
            pltpu.VMEM((FIX + 2 * EDGE, 128), F32),
            dma((8,)),
        ],
        compiler_params=pltpu.CompilerParams(vmem_limit_bytes=60 * 2**20),
        name="fix",
    )(starts, lengths, anchor, pre, hidden, normed, taps)


def solution(mesh):
    placed = (
        P(("grp", "seq"), "tp"),
        P(("grp", "seq"), "tp"),
        P(("grp", "seq"), "tp"),
        P("tp", None),
        P(("grp", "seq"), "tp"),
        P("tp"),
        P(None, "tp"),
        P("grp"),
        P("grp"),
    )
    return jax.shard_map(
        on_device, mesh=mesh, in_specs=placed, out_specs=P(("grp", "seq"), "tp"), check_vma=False
    )
```

```python
import functools

import jax
import jax.numpy as jnp
from jax import lax
from jax.experimental import pallas as pl
from jax.experimental.pallas import tpu as pltpu
from jax.sharding import PartitionSpec as P

HSIZE = 64
WIN = 128
KHALF = 15
REC = 8
KERNEL = 31
BLOCK = 128
CHUNK = 256
EDGE = 16
PHASES = 4
HALF = 64
COARSE = 16
STEPS = 9
FIX = 64
LANES = 256
EARLY, EARLY_SPAN, LATE_SPAN = 48, 40, 24
FILL = (2, 1, 1, 2)

F32 = jnp.float32
BF16 = jnp.bfloat16
MESH = pl.DeviceIdType.MESH


def label_of(positions, starts, lengths):
    label = jnp.full(positions.shape, -1, jnp.int32)
    for r in range(REC):
        first = starts[r]
        inside = (positions >= first) & (positions < first + lengths[r])
        label = jnp.where(inside, r, label)
    return label


def silu(total):
    return total * (F32(0.5) + F32(0.5) * jnp.tanh(total * F32(0.5)))


def half_pairs(a, b):
    keep = lax.broadcasted_iota(jnp.int32, a.shape, 1) < HALF
    return jnp.where(keep, a, pltpu.roll(b, HALF, 1)), jnp.where(keep, pltpu.roll(a, HALF, 1), b)


def spread_rows(cols, spots, span, wide, nb):
    reach = span + 2 * EDGE
    pitch = reach + 1
    for r, spot in enumerate(spots):
        low = spot // 16 * 16
        high = -(-(spot + reach) // 16) * 16
        block = nb[low:high, cols].astype(F32)
        wide[r * pitch : r * pitch + reach, :] = block[spot - low : spot - low + reach]


def direct(g, spots, span, wide, nb, taps_ref, emit):
    pitch = span + 2 * EDGE + 1
    cols = pl.ds(pl.multiple_of(g * 128, 128), 128)
    spread_rows(cols, spots, span, wide, nb)
    yield
    for r in range(0, len(spots), 2):
        places = [(r + i) * pitch + 8 * octet for i in range(2) for octet in range(span // 8)]
        totals = [None] * len(places)
        for tap in range(KERNEL):
            weight = jnp.broadcast_to(taps_ref[tap : tap + 1, cols], (8, 128))
            for i, place in enumerate(places):
                term = weight * wide[place + tap + 1 : place + tap + 9, :]
                totals[i] = term if tap == 0 else totals[i] + term
        emit(spots[r], cols, jnp.concatenate(totals, axis=0))
    yield
    yield


def convolve(g, spots, span, wide, padded, rows_of, shaped, weights, sums, eye_ref, nb, taps_ref, emit):
    units = span // PHASES
    pitch, step = span + 2 * EDGE + 1, span + 1
    cols = pl.ds(pl.multiple_of(g * 128, 128), 128)
    spread_rows(cols, spots, span, wide, nb)
    for u in range(units + STEPS - 1):
        at = [wide[pl.ds(PHASES * u + f, COARSE, stride=pitch), :] for f in range(PHASES)]
        low_a, high_a = half_pairs(at[0], at[1])
        low_b, high_b = half_pairs(at[2], at[3])
        rows = pl.ds(u * COARSE, COARSE)
        shaped[0, rows, 0:128] = low_a.astype(BF16)
        shaped[0, rows, 128:256] = low_b.astype(BF16)
        shaped[1, rows, 0:128] = high_a.astype(BF16)
        shaped[1, rows, 128:256] = high_b.astype(BF16)
    padded[8 : 8 + KERNEL, :] = taps_ref[:, cols]
    shifted = [padded[7 - p : 47 - p, :] for p in range(PHASES)]
    low_a, high_a = half_pairs(shifted[0], shifted[1])
    low_b, high_b = half_pairs(shifted[2], shifted[3])
    rows_of[0, :, 0:128] = low_a
    rows_of[0, :, 128:256] = low_b
    rows_of[1, :, 0:128] = high_a
    rows_of[1, :, 128:256] = high_b
    for h in range(2):
        for v in range(PHASES * STEPS):
            row = jnp.broadcast_to(rows_of[h, v : v + 1, :], (16, 256)).astype(BF16)
            for part in range(HALF // 16):
                weights[h, pl.ds(v * HALF + part * 16, 16), :] = row * eye_ref[pl.ds(part * 16, 16), :]
    yield
    results = []
    for h in range(2):
        left = jnp.concatenate(
            [shaped[h, pl.ds(s * COARSE, units * COARSE), :] for s in range(STEPS)], axis=1
        )
        results.append(jnp.dot(left, weights[h], preferred_element_type=F32))
    yield
    pair = half_pairs(results[0][:, :128], results[1][:, :128]) + half_pairs(
        results[0][:, 128:], results[1][:, 128:]
    )
    for p in range(PHASES):
        for u in range(units):
            sums[pl.ds(PHASES * u + p, COARSE, stride=step), :] = pair[p][u * COARSE : (u + 1) * COARSE]
    for r in range(0, len(spots), 2):
        parts = [sums[(r + i) * step : (r + i) * step + span, :] for i in range(2)]
        emit(spots[r], cols, jnp.concatenate(parts, axis=0))
    yield


def fix_kernel(
    starts, lengths, anchor_ref, pre_hbm, hid_hbm, nrm_hbm, taps_hbm, out_hbm,
    held, hidw, nrmw, outw, taps_ref, near, bases, sems, extra,
):
    frames, feats = pre_hbm.shape
    anchor = anchor_ref[0]
    pieces = sems.shape[0]
    whole = []
    for i in range(pieces):
        rows = pl.ds(i * (frames // pieces), frames // pieces)
        whole.append((
            pltpu.make_async_copy(pre_hbm.at[rows], held.at[rows], sems.at[i]),
            pltpu.make_async_copy(held.at[rows], out_hbm.at[rows], sems.at[i]),
        ))
        whole[-1][0].start()
    for fetch, store in whole:
        fetch.wait()
        store.start()
    def look(r, found):
        first = starts[r]
        close = starts[r - 1] + lengths[r - 1] + EDGE > first
        here = (first > anchor - EDGE) & (first < anchor + frames + EDGE)

        touching = close & here

        @pl.when(touching)
        def _():
            cut = first - anchor
            base = pl.multiple_of(jnp.clip((cut - EDGE) // 16 * 16, 0, frames - FIX), 16)
            bases[found] = base
            rows = pl.ds(base, FIX)
            fetch = (
                pltpu.make_async_copy(hid_hbm.at[rows], hidw, extra.at[0]),
                pltpu.make_async_copy(nrm_hbm.at[pl.ds(base, FIX + 2 * EDGE)], nrmw, extra.at[1]),
                pltpu.make_async_copy(taps_hbm, taps_ref, extra.at[2]),
            )
            for copy in fetch:
                copy.start()
            for copy in fetch:
                copy.wait()
            octets = base + 8 * lax.broadcasted_iota(jnp.int32, (FIX // 8, 128), 0)
            place = anchor + base + lax.broadcasted_iota(jnp.int32, (FIX, 1), 0)
            valid = label_of(place, starts, lengths) >= 0
            zero = jnp.zeros((FIX // 8, 128), F32)

            def column(g, inner):
                cols = pl.ds(pl.multiple_of(g * 128, 128), 128)
                near[...] = nrmw[:, cols].astype(F32)
                before = [zero] * 8
                after = [zero] * 8
                for offset in range(1, KERNEL + 8):
                    window = near[pl.ds(offset, FIX // 8, stride=8), :]
                    late = octets + (offset - EDGE) >= cut
                    window_after = jnp.where(late, window, zero)
                    window_before = jnp.where(late, zero, window)
                    for phase in range(8):
                        tap = offset - 1 - phase
                        if 0 <= tap < KERNEL:
                            weight = jnp.broadcast_to(taps_ref[tap : tap + 1, cols], (FIX // 8, 128))
                            before[phase] += weight * window_before
                            after[phase] += weight * window_after
                for phase in range(8):
                    late = octets + phase >= cut
                    near[pl.ds(phase, FIX // 8, stride=8), :] = jnp.where(late, after[phase], before[phase])
                total = jnp.where(valid, near[0:FIX, :], F32(0.0))
                outw[found, :, cols] = (hidw[:, cols] + silu(total)).astype(BF16)
                return inner

            lax.fori_loop(0, feats // 128, column, 0)

        return found + jnp.where(touching, 1, 0)

    found = lax.fori_loop(1, REC, look, jnp.int32(0))
    for fetch, store in whole:
        store.wait()

    def replace(i, carry):
        rows = pl.ds(pl.multiple_of(bases[i], 16), FIX)
        done = pltpu.make_async_copy(outw.at[i], out_hbm.at[rows], extra.at[0])
        done.start()
        done.wait()
        return carry

    lax.fori_loop(0, found, replace, 0)


def block_kernel(
    starts, lengths, q_hbm, k_hbm, v_hbm, w_hbm, res_hbm, gain_ref, taps_ref,
    pre_hbm, hid_hbm, nrm_hbm,
    qb, kb, kt, vb, wb, att, resb, hidb, nb, stat, peer,
    valid_ref, eye_ref, wide, padded, rows_of, shaped, taps_wide, sums,
    in_sem, send_sem, recv_sem, att_send, att_recv, stat_send, stat_recv, out_sem, pre_sem,
):
    frames, width = qb.shape
    feats = resb.shape[1]
    blocks, chunks = frames // BLOCK, frames // CHUNK
    seq, seqs = lax.axis_index("seq"), lax.axis_size("seq")
    tp = lax.axis_index("tp")
    other = 1 - tp
    has_left, has_right = seq > 0, seq < seqs - 1
    left, right = {"seq": seq - 1}, {"seq": seq + 1}
    mate = {"tp": other}

    def local(i, src, dst):
        return pltpu.make_async_copy(src, dst, in_sem.at[i])

    def remote(src, dst, i, to):
        return pltpu.make_async_remote_copy(
            src, dst, send_sem.at[i], recv_sem.at[i], device_id=to, device_id_type=MESH
        )

    def columns(owner):
        return pl.ds(pl.multiple_of(owner * feats, 128), feats)

    loads = (
        local(0, k_hbm, kb.at[pl.ds(WIN, frames)]),
        local(1, v_hbm, vb.at[pl.ds(WIN, frames)]),
        local(2, q_hbm, qb),
        local(3, w_hbm.at[:, columns(tp)], wb.at[tp]),
        local(4, res_hbm, resb),
    )
    for load in loads[:3]:
        load.start()

    barrier = pltpu.get_barrier_semaphore()
    pl.semaphore_signal(barrier, inc=1, device_id=mate, device_id_type=MESH)

    @pl.when(has_left)
    def _():
        pl.semaphore_signal(barrier, inc=1, device_id=left, device_id_type=MESH)

    @pl.when(has_right)
    def _():
        pl.semaphore_signal(barrier, inc=1, device_id=right, device_id_type=MESH)

    pl.semaphore_wait(barrier, 1 + jnp.minimum(seq, 1) + jnp.minimum(seqs - 1 - seq, 1))

    tail, head = pl.ds(frames - WIN, WIN), pl.ds(0, WIN)
    low, high = pl.ds(0, WIN), pl.ds(WIN + frames, WIN)
    to_right = (
        remote(k_hbm.at[tail], kb.at[low], 0, right),
        remote(v_hbm.at[tail], vb.at[low], 1, right),
    )
    to_left = (
        remote(k_hbm.at[head], kb.at[high], 2, left),
        remote(v_hbm.at[head], vb.at[high], 3, left),
    )
    to_mate = remote(w_hbm.at[:, columns(other)], wb.at[tp], 4, mate)

    @pl.when(has_right)
    def _():
        for copy in to_right:
            copy.start()

    to_mate.start()

    @pl.when(jnp.logical_not(has_left))
    def _():
        kt[:, low] = jnp.zeros((width, WIN), BF16)
        vb[low] = jnp.zeros((WIN, width), BF16)

    @pl.when(jnp.logical_not(has_right))
    def _():
        kt[:, high] = jnp.zeros((width, WIN), BF16)
        vb[high] = jnp.zeros((WIN, width), BF16)

    def turn(i, carry):
        part = pl.ds(pl.multiple_of(i * 128, 128), 128)
        for pair in range(width // 128):
            lanes = pl.ds(pair * 128, 128)
            kt[lanes, part] = jnp.transpose(kb[part, lanes])
        return carry

    anchor = seq * frames
    place = anchor + lax.broadcasted_iota(jnp.int32, (frames, 128), 0)
    inside = place < 0
    for r in range(REC):
        inside |= (place >= starts[r]) & (place < starts[r] + lengths[r])
    valid_ref[...] = jnp.where(inside, F32(1.0), F32(0.0))
    fold = lax.broadcasted_iota(jnp.int32, (HALF, 256), 1) % HALF
    down = lax.broadcasted_iota(jnp.int32, (HALF, 256), 0)
    eye_ref[...] = jnp.where(fold == down, F32(1.0), F32(0.0)).astype(BF16)
    padded[...] = jnp.zeros_like(padded)

    loads[0].wait()
    lax.fori_loop(1, 1 + frames // 128, turn, 0)
    for load in loads[1:3]:
        load.wait()
    for load in loads[3:]:
        load.start()

    span = BLOCK + 2 * WIN

    def att_copy(b):
        rows = pl.ds(pl.multiple_of(b * BLOCK, BLOCK), BLOCK)
        return pltpu.make_async_remote_copy(
            att.at[tp, rows], att.at[tp, rows], att_send.at[b], att_recv.at[b],
            device_id=mate, device_id_type=MESH,
        )

    def attend(b):
        row = pl.multiple_of(b * BLOCK, BLOCK)
        rows = pl.ds(row, BLOCK)
        keys = pl.ds(row, span)
        q_pos = lax.broadcasted_iota(jnp.int32, (BLOCK, 1), 0)
        k_pos = lax.broadcasted_iota(jnp.int32, (1, span), 1)
        q_seg = label_of(anchor + row + q_pos, starts, lengths)
        k_seg = label_of(anchor + row - WIN + k_pos, starts, lengths)
        gap = k_pos - q_pos
        allowed = (gap >= 0) & (gap <= 2 * WIN) & (q_seg == k_seg) & (q_seg >= 0)
        bias = jnp.where(allowed, F32(0.0), F32(-1e30)).astype(BF16)
        valid = q_seg >= 0
        down = lax.broadcasted_iota(jnp.int32, (BLOCK, BLOCK), 0)
        across = lax.broadcasted_iota(jnp.int32, (BLOCK, BLOCK), 1)
        eye = jnp.where(down == across, F32(1.0), F32(0.0)).astype(BF16)
        first = lax.broadcasted_iota(jnp.int32, (span, 128), 1) < HSIZE
        ones = (
            jnp.where(first, F32(1.0), F32(0.0)).astype(BF16),
            jnp.where(first, F32(0.0), F32(1.0)).astype(BF16),
        )
        gap_rows = jnp.zeros((HSIZE, span), BF16)
        for pair in range(width // 128):
            lanes = pl.ds(pair * 128, 128)
            left_side = jnp.concatenate([qb[rows, lanes] * BF16(HSIZE**-0.5), eye], axis=1)
            turned = kt[lanes, keys]
            right_side = jnp.concatenate(
                [
                    jnp.concatenate([turned[:HSIZE], gap_rows, bias], axis=0),
                    jnp.concatenate([gap_rows, turned[HSIZE:], bias], axis=0),
                ],
                axis=1,
            )
            scores = jnp.dot(left_side, right_side, preferred_element_type=F32)
            weights = []
            for own in (scores[:, :span], scores[:, span:]):
                weights.append(jnp.exp(own - jnp.max(own, axis=1, keepdims=True)).astype(BF16))
            v = vb[keys, lanes]
            zero = jnp.zeros_like(v)
            values = jnp.concatenate(
                [
                    jnp.concatenate([jnp.where(first, v, zero), ones[0]], axis=1),
                    jnp.concatenate([jnp.where(first, zero, v), ones[1]], axis=1),
                ],
                axis=0,
            )
            mixed = jnp.dot(jnp.concatenate(weights, axis=1), values, preferred_element_type=F32)
            mixed = mixed[:, :128] / mixed[:, 128:]
            att[tp, rows, lanes] = jnp.where(valid, mixed, F32(0.0)).astype(BF16)
        att_copy(b).start()

    def inner(b, carry):
        attend(b)

        return carry

    lax.fori_loop(1, blocks - 1, inner, 0)

    loads[3].wait()
    to_mate.wait_recv()
    loads[4].wait()

    def stat_copy(c):
        rows = pl.ds(pl.multiple_of(c * CHUNK, CHUNK), CHUNK)
        return pltpu.make_async_remote_copy(
            stat.at[rows], peer.at[rows], stat_send.at[c], stat_recv.at[c],
            device_id=mate, device_id_type=MESH,
        )

    def hid_copy(c):
        rows = pl.ds(pl.multiple_of(c * CHUNK, CHUNK), CHUNK)
        return pltpu.make_async_copy(hidb.at[rows], hid_hbm.at[rows], out_sem.at[c])

    def nrm_copy(c):
        rows = pl.ds(pl.multiple_of(EDGE + c * CHUNK, EDGE), CHUNK)
        return pltpu.make_async_copy(nb.at[rows], nrm_hbm.at[rows], out_sem.at[chunks + c])

    chunk_lane = lax.broadcasted_iota(jnp.int32, (CHUNK, 128), 1)
    tile = min(512, feats)

    def project(c):
        for part in range(CHUNK // BLOCK):
            att_copy(c * (CHUNK // BLOCK) + part).wait_recv()
        rows = pl.ds(pl.multiple_of(c * CHUNK, CHUNK), CHUNK)
        total = jnp.zeros((CHUNK, 1), F32)
        for t in range(feats // tile):
            cols = pl.ds(t * tile, tile)
            hidden = resb[rows, cols].astype(F32)
            for part in range(2):
                hidden += jnp.dot(att[part, rows], wb[part, :, cols], preferred_element_type=F32)
            hidb[rows, cols] = hidden
            total += jnp.sum(hidden, axis=1, keepdims=True)
        mean = total * F32(1.0 / feats)
        spread = jnp.zeros((CHUNK, 1), F32)
        for t in range(feats // tile):
            centered = hidb[rows, pl.ds(t * tile, tile)] - mean
            spread += jnp.sum(centered * centered, axis=1, keepdims=True)
        stat[rows] = jnp.where(chunk_lane < 64, mean, spread)
        stat_copy(c).start()
        hid_copy(c).start()

    first_rows, last_rows = pl.ds(EDGE, EDGE), pl.ds(frames, EDGE)
    low_edge, high_edge = pl.ds(0, EDGE), pl.ds(frames + EDGE, EDGE)
    edge_right = remote(nb.at[last_rows], nb.at[low_edge], 5, right)
    edge_left = remote(nb.at[first_rows], nb.at[high_edge], 6, left)

    def normalise(c):
        stat_copy(c).wait_recv()
        row = pl.multiple_of(c * CHUNK, CHUNK)
        rows = pl.ds(row, CHUNK)
        mine, theirs = stat[rows], peer[rows]
        mean_a, mean_b = mine[:, 0:1], theirs[:, 0:1]
        spread = mine[:, 64:65] + theirs[:, 64:65]
        shift = mean_a - mean_b
        variance = (spread + shift * shift * F32(feats / 2)) * F32(1.0 / (2 * feats))
        mean = (mean_a + mean_b) * F32(0.5)
        scale = lax.rsqrt(variance + F32(1e-05)) * valid_ref[rows, 0:1]
        for t in range(feats // tile):
            cols = pl.ds(t * tile, tile)
            normed = (hidb[rows, cols] - mean) * scale * gain_ref[cols][None, :]
            nb[pl.ds(pl.multiple_of(row + EDGE, EDGE), CHUNK), cols] = normed.astype(BF16)
        nrm_copy(c).start()

    project(jnp.int32(1))

    @pl.when(has_right)
    def _():
        for copy in to_right:
            copy.wait_send()

    @pl.when(has_left)
    def _():
        for copy in to_left:
            copy.start()

    project(jnp.int32(2))
    normalise(jnp.int32(1))

    @pl.when(has_left)
    def _():
        for copy in to_right:
            copy.wait_recv()
        turn(0, 0)

    attend(jnp.int32(0))
    normalise(jnp.int32(2))
    project(jnp.int32(0))
    normalise(jnp.int32(0))

    @pl.when(has_left)
    def _():
        edge_left.start()

    tail_rows = frames - EARLY - COARSE * EARLY_SPAN
    early = [EARLY + EARLY_SPAN * r for r in range(COARSE)]
    late = [EARLY + COARSE * EARLY_SPAN + LATE_SPAN * r for r in range(tail_rows // LATE_SPAN)]
    late += [LATE_SPAN * r for r in range(EARLY // LATE_SPAN)]

    def emit(spot, cols, total):
        rows = pl.ds(spot, total.shape[0])
        resb[rows, cols] = (hidb[rows, cols] + silu(total * valid_ref[rows, :])).astype(BF16)

    def both(spots, size, vector):
        def run(i, carry):
            tasks = []
            for half in range(2):
                if half in vector:
                    tasks.append(direct(i * 2 + half, spots, size, wide.at[half], nb, taps_ref, emit))
                else:
                    tasks.append(convolve(
                        i * 2 + half, spots, size, wide.at[half], padded.at[half], rows_of.at[half],
                        shaped.at[half], taps_wide.at[half], sums.at[half], eye_ref, nb, taps_ref, emit,
                    ))
            for _ in range(3):
                for task in tasks:
                    next(task)
            return carry

        return run

    early_step, late_step = both(early, EARLY_SPAN, ()), both(late, LATE_SPAN, (0, 1))
    stops = [sum(FILL[:i]) for i in range(len(FILL) + 1)]

    def fill(i):
        lax.fori_loop(stops[i], stops[i + 1], early_step, 0)

    fill(0)

    @pl.when(has_right)
    def _():
        for copy in to_left:
            copy.wait_recv()
        turn(1 + frames // 128, 0)

    attend(jnp.int32(blocks - 1))
    fill(1)
    project(jnp.int32(chunks - 1))
    fill(2)
    normalise(jnp.int32(chunks - 1))

    @pl.when(has_right)
    def _():
        edge_right.start()

    fill(3)

    @pl.when(has_left)
    def _():
        edge_right.wait_recv()

    @pl.when(jnp.logical_not(has_left))
    def _():
        nb[low_edge] = jnp.zeros((EDGE, feats), BF16)

    @pl.when(has_right)
    def _():
        edge_left.wait_recv()

    @pl.when(jnp.logical_not(has_right))
    def _():
        nb[high_edge] = jnp.zeros((EDGE, feats), BF16)

    edges = (
        pltpu.make_async_copy(nb.at[low_edge], nrm_hbm.at[low_edge], out_sem.at[2 * chunks]),
        pltpu.make_async_copy(nb.at[high_edge], nrm_hbm.at[high_edge], out_sem.at[2 * chunks + 1]),
    )
    for copy in edges:
        copy.start()

    def pre_copy(i):
        cols = pl.ds(pl.multiple_of(i * LANES, LANES), LANES)
        return pltpu.make_async_copy(resb.at[:, cols], pre_hbm.at[:, cols], pre_sem.at[i])

    def finish(i, carry):
        late_step(i, 0)
        pre_copy(i).start()
        return carry

    lax.fori_loop(0, feats // LANES, finish, 0)

    @pl.when(has_right)
    def _():
        edge_right.wait_send()

    @pl.when(has_left)
    def _():
        for copy in (*to_left, edge_left):
            copy.wait_send()

    to_mate.wait_send()

    def drain(c, carry):
        stat_copy(c).wait_send()
        hid_copy(c).wait()
        nrm_copy(c).wait()
        for part in range(CHUNK // BLOCK):
            att_copy(c * (CHUNK // BLOCK) + part).wait_send()
        return carry

    lax.fori_loop(0, chunks, drain, 0)

    def leave(i, carry):
        pre_copy(i).wait()
        return carry

    lax.fori_loop(0, feats // LANES, leave, 0)
    for copy in edges:
        copy.wait()


def on_device(q, k, v, weight, residual, gain, taps, starts, lengths):
    frames, width = q.shape
    feats = residual.shape[1]
    chunks, blocks = frames // CHUNK, frames // BLOCK
    anywhere = pl.BlockSpec(memory_space=pl.ANY)
    scalars = pl.BlockSpec(memory_space=pltpu.SMEM)
    dma = pltpu.SemaphoreType.DMA
    tall = (max(EARLY_SPAN, LATE_SPAN) // PHASES + STEPS - 1) * COARSE
    pre, hidden, normed = pl.pallas_call(
        block_kernel,
        out_shape=(
            jax.ShapeDtypeStruct((frames, feats), BF16),
            jax.ShapeDtypeStruct((frames, feats), F32),
            jax.ShapeDtypeStruct((frames + 2 * EDGE, feats), BF16),
        ),
        in_specs=[scalars, scalars] + [anywhere] * 5 + [pl.BlockSpec(memory_space=pltpu.VMEM)] * 2,
        out_specs=(anywhere,) * 3,
        scratch_shapes=[
            pltpu.VMEM((frames, width), BF16),
            pltpu.VMEM((frames + 2 * WIN, width), BF16),
            pltpu.VMEM((width, frames + 2 * WIN), BF16),
            pltpu.VMEM((frames + 2 * WIN, width), BF16),
            pltpu.VMEM((2, width, feats), BF16),
            pltpu.VMEM((2, frames, width), BF16),
            pltpu.VMEM((frames, feats), BF16),
            pltpu.VMEM((frames, feats), F32),
            pltpu.VMEM((frames + 2 * EDGE, feats), BF16),
            pltpu.VMEM((frames, 128), F32),
            pltpu.VMEM((frames, 128), F32),
            pltpu.VMEM((frames, 128), F32),
            pltpu.VMEM((HALF, 256), BF16),
            pltpu.VMEM((2, COARSE * (EARLY_SPAN + 2 * EDGE + 1), 128), F32),
            pltpu.VMEM((2, 48, 128), F32),
            pltpu.VMEM((2, 2, 40, 256), F32),
            pltpu.VMEM((2, 2, tall, 256), BF16),
            pltpu.VMEM((2, 2, PHASES * STEPS * HALF, 256), BF16),
            pltpu.VMEM((2, COARSE * (EARLY_SPAN + 1), 128), F32),
            dma((5,)), dma((7,)), dma((7,)), dma((blocks,)), dma((blocks,)),
            dma((chunks,)), dma((chunks,)), dma((2 * chunks + 2,)), dma((feats // LANES,)),
        ],
        compiler_params=pltpu.CompilerParams(
            collective_id=0, has_side_effects=True, vmem_limit_bytes=60 * 2**20
        ),
        name="mix",
    )(starts, lengths, q, k, v, weight, residual, gain, taps)
    anchor = (lax.axis_index("seq") * frames).astype(jnp.int32).reshape(1)
    return pl.pallas_call(
        fix_kernel,
        out_shape=jax.ShapeDtypeStruct((frames, feats), BF16),
        in_specs=[scalars] * 3 + [anywhere] * 4,
        out_specs=anywhere,
        scratch_shapes=[
            pltpu.VMEM((frames, feats), BF16),
            pltpu.VMEM((FIX, feats), F32),
            pltpu.VMEM((FIX + 2 * EDGE, feats), BF16),
            pltpu.VMEM((REC, FIX, feats), BF16),
            pltpu.VMEM((KERNEL, feats), F32),
            pltpu.VMEM((FIX + 2 * EDGE, 128), F32),
            pltpu.SMEM((REC,), jnp.int32),
            dma((8,)), dma((3,)),
        ],
        compiler_params=pltpu.CompilerParams(vmem_limit_bytes=60 * 2**20),
        name="fix",
    )(starts, lengths, anchor, pre, hidden, normed, taps)


def solution(mesh):
    placed = (
        P(("grp", "seq"), "tp"),
        P(("grp", "seq"), "tp"),
        P(("grp", "seq"), "tp"),
        P("tp", None),
        P(("grp", "seq"), "tp"),
        P("tp"),
        P(None, "tp"),
        P("grp"),
        P("grp"),
    )
    return jax.shard_map(
        on_device, mesh=mesh, in_specs=placed, out_specs=P(("grp", "seq"), "tp"), check_vma=False
    )
```

```python
import functools

import jax
import jax.numpy as jnp
from jax import lax
from jax.experimental import pallas as pl
from jax.experimental.pallas import tpu as pltpu
from jax.sharding import PartitionSpec as P

HSIZE = 64
WIN = 128
KHALF = 15
REC = 8
KERNEL = 31
BLOCK = 128
CHUNK = 256
EDGE = 16
PHASES = 4
HALF = 64
COARSE = 16
STEPS = 9
FIX = 64
LANES = 256
EARLY, EARLY_SPAN, LATE_SPAN = 48, 40, 24
FILL = (2, 1, 1, 2)

F32 = jnp.float32
BF16 = jnp.bfloat16
MESH = pl.DeviceIdType.MESH


def label_of(positions, starts, lengths):
    label = jnp.full(positions.shape, -1, jnp.int32)
    for r in range(REC):
        first = starts[r]
        inside = (positions >= first) & (positions < first + lengths[r])
        label = jnp.where(inside, r, label)
    return label


def silu(total):
    return total * (F32(0.5) + F32(0.5) * jnp.tanh(total * F32(0.5)))


def half_pairs(a, b):
    keep = lax.broadcasted_iota(jnp.int32, a.shape, 1) < HALF
    return jnp.where(keep, a, pltpu.roll(b, HALF, 1)), jnp.where(keep, pltpu.roll(a, HALF, 1), b)


def spread_rows(cols, spots, span, wide, nb):
    reach = span + 2 * EDGE
    pitch = reach + 1
    for r, spot in enumerate(spots):
        low = spot // 16 * 16
        high = -(-(spot + reach) // 16) * 16
        block = nb[low:high, cols].astype(F32)
        wide[r * pitch : r * pitch + reach, :] = block[spot - low : spot - low + reach]


def direct(g, spots, span, wide, nb, taps_ref, emit):
    pitch = span + 2 * EDGE + 1
    cols = pl.ds(pl.multiple_of(g * 128, 128), 128)
    spread_rows(cols, spots, span, wide, nb)
    yield
    for r in range(0, len(spots), 2):
        places = [(r + i) * pitch + 8 * octet for i in range(2) for octet in range(span // 8)]
        totals = [None] * len(places)
        for tap in range(KERNEL):
            weight = jnp.broadcast_to(taps_ref[tap : tap + 1, cols], (8, 128))
            for i, place in enumerate(places):
                term = weight * wide[place + tap + 1 : place + tap + 9, :]
                totals[i] = term if tap == 0 else totals[i] + term
        emit(spots[r], cols, jnp.concatenate(totals, axis=0))
    yield
    yield


def convolve(g, spots, span, wide, padded, rows_of, shaped, weights, sums, eye_ref, nb, taps_ref, emit):
    units = span // PHASES
    pitch, step = span + 2 * EDGE + 1, span + 1
    cols = pl.ds(pl.multiple_of(g * 128, 128), 128)
    spread_rows(cols, spots, span, wide, nb)
    for u in range(units + STEPS - 1):
        at = [wide[pl.ds(PHASES * u + f, COARSE, stride=pitch), :] for f in range(PHASES)]
        low_a, high_a = half_pairs(at[0], at[1])
        low_b, high_b = half_pairs(at[2], at[3])
        rows = pl.ds(u * COARSE, COARSE)
        shaped[0, rows, 0:128] = low_a.astype(BF16)
        shaped[0, rows, 128:256] = low_b.astype(BF16)
        shaped[1, rows, 0:128] = high_a.astype(BF16)
        shaped[1, rows, 128:256] = high_b.astype(BF16)
    padded[8 : 8 + KERNEL, :] = taps_ref[:, cols]
    shifted = [padded[7 - p : 47 - p, :] for p in range(PHASES)]
    low_a, high_a = half_pairs(shifted[0], shifted[1])
    low_b, high_b = half_pairs(shifted[2], shifted[3])
    rows_of[0, :, 0:128] = low_a
    rows_of[0, :, 128:256] = low_b
    rows_of[1, :, 0:128] = high_a
    rows_of[1, :, 128:256] = high_b
    for h in range(2):
        for v in range(PHASES * STEPS):
            row = jnp.broadcast_to(rows_of[h, v : v + 1, :], (16, 256)).astype(BF16)
            for part in range(HALF // 16):
                weights[h, pl.ds(v * HALF + part * 16, 16), :] = row * eye_ref[pl.ds(part * 16, 16), :]
    yield
    results = []
    for h in range(2):
        left = jnp.concatenate(
            [shaped[h, pl.ds(s * COARSE, units * COARSE), :] for s in range(STEPS)], axis=1
        )
        results.append(jnp.dot(left, weights[h], preferred_element_type=F32))
    yield
    pair = half_pairs(results[0][:, :128], results[1][:, :128]) + half_pairs(
        results[0][:, 128:], results[1][:, 128:]
    )
    for p in range(PHASES):
        for u in range(units):
            sums[pl.ds(PHASES * u + p, COARSE, stride=step), :] = pair[p][u * COARSE : (u + 1) * COARSE]
    for r in range(0, len(spots), 2):
        parts = [sums[(r + i) * step : (r + i) * step + span, :] for i in range(2)]
        emit(spots[r], cols, jnp.concatenate(parts, axis=0))
    yield


def fix_kernel(
    starts, lengths, anchor_ref, pre_hbm, hid_hbm, nrm_hbm, taps_hbm, out_hbm,
    held, hidw, nrmw, outw, taps_ref, near, bases, sems, extra,
):
    frames, feats = pre_hbm.shape
    anchor = anchor_ref[0]
    pieces = sems.shape[0]
    whole = []
    for i in range(pieces):
        rows = pl.ds(i * (frames // pieces), frames // pieces)
        whole.append((
            pltpu.make_async_copy(pre_hbm.at[rows], held.at[rows], sems.at[i]),
            pltpu.make_async_copy(held.at[rows], out_hbm.at[rows], sems.at[i]),
        ))
        whole[-1][0].start()
    def forward():
        for fetch, store in whole:
            fetch.wait()
            store.start()

    def look(r, found):
        first = starts[r]
        close = starts[r - 1] + lengths[r - 1] + EDGE > first
        here = (first > anchor - EDGE) & (first < anchor + frames + EDGE)

        touching = close & here

        @pl.when(touching)
        def _():
            cut = first - anchor
            base = pl.multiple_of(jnp.clip((cut - EDGE) // 16 * 16, 0, frames - FIX), 16)
            bases[found] = base
            rows = pl.ds(base, FIX)
            fetch = (
                pltpu.make_async_copy(hid_hbm.at[rows], hidw, extra.at[0]),
                pltpu.make_async_copy(nrm_hbm.at[pl.ds(base, FIX + 2 * EDGE)], nrmw, extra.at[1]),
                pltpu.make_async_copy(taps_hbm, taps_ref, extra.at[2]),
            )
            for copy in fetch:
                copy.start()
            for copy in fetch:
                copy.wait()

            @pl.when(found == 0)
            def _():
                forward()

            octets = base + 8 * lax.broadcasted_iota(jnp.int32, (FIX // 8, 128), 0)
            place = anchor + base + lax.broadcasted_iota(jnp.int32, (FIX, 1), 0)
            valid = label_of(place, starts, lengths) >= 0
            zero = jnp.zeros((FIX // 8, 128), F32)
            sides = [octets + phase >= cut for phase in range(8)]

            def column(g, inner):
                cols = pl.ds(pl.multiple_of(g * 128, 128), 128)
                near[...] = nrmw[:, cols].astype(F32)
                totals = [zero] * 8
                for offset in range(1, KERNEL + 8):
                    window = near[pl.ds(offset, FIX // 8, stride=8), :]
                    late = octets + (offset - EDGE) >= cut
                    window_after = jnp.where(late, window, zero)
                    window_before = jnp.where(late, zero, window)
                    for phase in range(8):
                        tap = offset - 1 - phase
                        if 0 <= tap < KERNEL:
                            weight = jnp.broadcast_to(taps_ref[tap : tap + 1, cols], (FIX // 8, 128))
                            totals[phase] += weight * jnp.where(sides[phase], window_after, window_before)
                for phase in range(8):
                    near[pl.ds(phase, FIX // 8, stride=8), :] = totals[phase]
                total = jnp.where(valid, near[0:FIX, :], F32(0.0))
                outw[found, :, cols] = (hidw[:, cols] + silu(total)).astype(BF16)
                return inner

            lax.fori_loop(0, feats // 128, column, 0)

        return found + jnp.where(touching, 1, 0)

    found = lax.fori_loop(1, REC, look, jnp.int32(0))
    pl.when(found == 0)(forward)
    for fetch, store in whole:
        store.wait()

    def replace(i, carry):
        rows = pl.ds(pl.multiple_of(bases[i], 16), FIX)
        done = pltpu.make_async_copy(outw.at[i], out_hbm.at[rows], extra.at[0])
        done.start()
        done.wait()
        return carry

    lax.fori_loop(0, found, replace, 0)


def block_kernel(
    starts, lengths, q_hbm, k_hbm, v_hbm, w_hbm, res_hbm, gain_ref, taps_ref,
    pre_hbm, hid_hbm, nrm_hbm,
    qb, kb, kt, vb, wb, att, resb, hidb, nb, stat, peer,
    valid_ref, eye_ref, wide, padded, rows_of, shaped, taps_wide, sums,
    in_sem, send_sem, recv_sem, att_send, att_recv, stat_send, stat_recv, out_sem, pre_sem,
):
    frames, width = qb.shape
    feats = resb.shape[1]
    blocks, chunks = frames // BLOCK, frames // CHUNK
    seq, seqs = lax.axis_index("seq"), lax.axis_size("seq")
    tp = lax.axis_index("tp")
    other = 1 - tp
    has_left, has_right = seq > 0, seq < seqs - 1
    left, right = {"seq": seq - 1}, {"seq": seq + 1}
    mate = {"tp": other}

    def local(i, src, dst):
        return pltpu.make_async_copy(src, dst, in_sem.at[i])

    def remote(src, dst, i, to):
        return pltpu.make_async_remote_copy(
            src, dst, send_sem.at[i], recv_sem.at[i], device_id=to, device_id_type=MESH
        )

    def columns(owner):
        return pl.ds(pl.multiple_of(owner * feats, 128), feats)

    loads = (
        local(0, k_hbm, kb.at[pl.ds(WIN, frames)]),
        local(1, v_hbm, vb.at[pl.ds(WIN, frames)]),
        local(2, q_hbm, qb),
        local(3, w_hbm.at[:, columns(tp)], wb.at[tp]),
        local(4, res_hbm, resb),
    )
    for load in loads[:3]:
        load.start()

    barrier = pltpu.get_barrier_semaphore()
    pl.semaphore_signal(barrier, inc=1, device_id=mate, device_id_type=MESH)

    @pl.when(has_left)
    def _():
        pl.semaphore_signal(barrier, inc=1, device_id=left, device_id_type=MESH)

    @pl.when(has_right)
    def _():
        pl.semaphore_signal(barrier, inc=1, device_id=right, device_id_type=MESH)

    pl.semaphore_wait(barrier, 1 + jnp.minimum(seq, 1) + jnp.minimum(seqs - 1 - seq, 1))

    tail, head = pl.ds(frames - WIN, WIN), pl.ds(0, WIN)
    low, high = pl.ds(0, WIN), pl.ds(WIN + frames, WIN)
    to_right = (
        remote(k_hbm.at[tail], kb.at[low], 0, right),
        remote(v_hbm.at[tail], vb.at[low], 1, right),
    )
    to_left = (
        remote(k_hbm.at[head], kb.at[high], 2, left),
        remote(v_hbm.at[head], vb.at[high], 3, left),
    )
    to_mate = remote(w_hbm.at[:, columns(other)], wb.at[tp], 4, mate)

    @pl.when(has_right)
    def _():
        for copy in to_right:
            copy.start()

    to_mate.start()

    @pl.when(jnp.logical_not(has_left))
    def _():
        kt[:, low] = jnp.zeros((width, WIN), BF16)
        vb[low] = jnp.zeros((WIN, width), BF16)

    @pl.when(jnp.logical_not(has_right))
    def _():
        kt[:, high] = jnp.zeros((width, WIN), BF16)
        vb[high] = jnp.zeros((WIN, width), BF16)

    def turn(i, carry):
        part = pl.ds(pl.multiple_of(i * 128, 128), 128)
        for pair in range(width // 128):
            lanes = pl.ds(pair * 128, 128)
            kt[lanes, part] = jnp.transpose(kb[part, lanes])
        return carry

    anchor = seq * frames
    place = anchor + lax.broadcasted_iota(jnp.int32, (frames, 128), 0)
    inside = place < 0
    for r in range(REC):
        inside |= (place >= starts[r]) & (place < starts[r] + lengths[r])
    valid_ref[...] = jnp.where(inside, F32(1.0), F32(0.0))
    fold = lax.broadcasted_iota(jnp.int32, (HALF, 256), 1) % HALF
    down = lax.broadcasted_iota(jnp.int32, (HALF, 256), 0)
    eye_ref[...] = jnp.where(fold == down, F32(1.0), F32(0.0)).astype(BF16)
    padded[...] = jnp.zeros_like(padded)

    loads[0].wait()
    lax.fori_loop(1, 1 + frames // 128, turn, 0)
    for load in loads[1:3]:
        load.wait()
    for load in loads[3:]:
        load.start()

    span = BLOCK + 2 * WIN

    def att_copy(b):
        rows = pl.ds(pl.multiple_of(b * BLOCK, BLOCK), BLOCK)
        return pltpu.make_async_remote_copy(
            att.at[tp, rows], att.at[tp, rows], att_send.at[b], att_recv.at[b],
            device_id=mate, device_id_type=MESH,
        )

    def attend(b):
        row = pl.multiple_of(b * BLOCK, BLOCK)
        rows = pl.ds(row, BLOCK)
        keys = pl.ds(row, span)
        q_pos = lax.broadcasted_iota(jnp.int32, (BLOCK, 1), 0)
        k_pos = lax.broadcasted_iota(jnp.int32, (1, span), 1)
        q_seg = label_of(anchor + row + q_pos, starts, lengths)
        k_seg = label_of(anchor + row - WIN + k_pos, starts, lengths)
        gap = k_pos - q_pos
        allowed = (gap >= 0) & (gap <= 2 * WIN) & (q_seg == k_seg) & (q_seg >= 0)
        bias = jnp.where(allowed, F32(0.0), F32(-1e30)).astype(BF16)
        valid = q_seg >= 0
        down = lax.broadcasted_iota(jnp.int32, (BLOCK, BLOCK), 0)
        across = lax.broadcasted_iota(jnp.int32, (BLOCK, BLOCK), 1)
        eye = jnp.where(down == across, F32(1.0), F32(0.0)).astype(BF16)
        first = lax.broadcasted_iota(jnp.int32, (span, 128), 1) < HSIZE
        ones = (
            jnp.where(first, F32(1.0), F32(0.0)).astype(BF16),
            jnp.where(first, F32(0.0), F32(1.0)).astype(BF16),
        )
        gap_rows = jnp.zeros((HSIZE, span), BF16)
        for pair in range(width // 128):
            lanes = pl.ds(pair * 128, 128)
            left_side = jnp.concatenate([qb[rows, lanes] * BF16(HSIZE**-0.5), eye], axis=1)
            turned = kt[lanes, keys]
            right_side = jnp.concatenate(
                [
                    jnp.concatenate([turned[:HSIZE], gap_rows, bias], axis=0),
                    jnp.concatenate([gap_rows, turned[HSIZE:], bias], axis=0),
                ],
                axis=1,
            )
            scores = jnp.dot(left_side, right_side, preferred_element_type=F32)
            weights = []
            for own in (scores[:, :span], scores[:, span:]):
                weights.append(jnp.exp(own - jnp.max(own, axis=1, keepdims=True)).astype(BF16))
            v = vb[keys, lanes]
            zero = jnp.zeros_like(v)
            values = jnp.concatenate(
                [
                    jnp.concatenate([jnp.where(first, v, zero), ones[0]], axis=1),
                    jnp.concatenate([jnp.where(first, zero, v), ones[1]], axis=1),
                ],
                axis=0,
            )
            mixed = jnp.dot(jnp.concatenate(weights, axis=1), values, preferred_element_type=F32)
            mixed = mixed[:, :128] / mixed[:, 128:]
            att[tp, rows, lanes] = jnp.where(valid, mixed, F32(0.0)).astype(BF16)
        att_copy(b).start()

    def inner(b, carry):
        attend(b)

        return carry

    lax.fori_loop(1, blocks - 1, inner, 0)

    loads[3].wait()
    to_mate.wait_recv()
    loads[4].wait()

    def stat_copy(c):
        rows = pl.ds(pl.multiple_of(c * CHUNK, CHUNK), CHUNK)
        return pltpu.make_async_remote_copy(
            stat.at[rows], peer.at[rows], stat_send.at[c], stat_recv.at[c],
            device_id=mate, device_id_type=MESH,
        )

    def hid_copy(c):
        rows = pl.ds(pl.multiple_of(c * CHUNK, CHUNK), CHUNK)
        return pltpu.make_async_copy(hidb.at[rows], hid_hbm.at[rows], out_sem.at[c])

    def nrm_copy(c):
        rows = pl.ds(pl.multiple_of(EDGE + c * CHUNK, EDGE), CHUNK)
        return pltpu.make_async_copy(nb.at[rows], nrm_hbm.at[rows], out_sem.at[chunks + c])

    chunk_lane = lax.broadcasted_iota(jnp.int32, (CHUNK, 128), 1)
    tile = min(512, feats)

    def project(c):
        for part in range(CHUNK // BLOCK):
            att_copy(c * (CHUNK // BLOCK) + part).wait_recv()
        rows = pl.ds(pl.multiple_of(c * CHUNK, CHUNK), CHUNK)
        total = jnp.zeros((CHUNK, 1), F32)
        for t in range(feats // tile):
            cols = pl.ds(t * tile, tile)
            hidden = resb[rows, cols].astype(F32)
            for part in range(2):
                hidden += jnp.dot(att[part, rows], wb[part, :, cols], preferred_element_type=F32)
            hidb[rows, cols] = hidden
            total += jnp.sum(hidden, axis=1, keepdims=True)
        mean = total * F32(1.0 / feats)
        spread = jnp.zeros((CHUNK, 1), F32)
        for t in range(feats // tile):
            centered = hidb[rows, pl.ds(t * tile, tile)] - mean
            spread += jnp.sum(centered * centered, axis=1, keepdims=True)
        stat[rows] = jnp.where(chunk_lane < 64, mean, spread)
        stat_copy(c).start()
        hid_copy(c).start()

    first_rows, last_rows = pl.ds(EDGE, EDGE), pl.ds(frames, EDGE)
    low_edge, high_edge = pl.ds(0, EDGE), pl.ds(frames + EDGE, EDGE)
    edge_right = remote(nb.at[last_rows], nb.at[low_edge], 5, right)
    edge_left = remote(nb.at[first_rows], nb.at[high_edge], 6, left)

    def normalise(c):
        stat_copy(c).wait_recv()
        row = pl.multiple_of(c * CHUNK, CHUNK)
        rows = pl.ds(row, CHUNK)
        mine, theirs = stat[rows], peer[rows]
        mean_a, mean_b = mine[:, 0:1], theirs[:, 0:1]
        spread = mine[:, 64:65] + theirs[:, 64:65]
        shift = mean_a - mean_b
        variance = (spread + shift * shift * F32(feats / 2)) * F32(1.0 / (2 * feats))
        mean = (mean_a + mean_b) * F32(0.5)
        scale = lax.rsqrt(variance + F32(1e-05)) * valid_ref[rows, 0:1]
        for t in range(feats // tile):
            cols = pl.ds(t * tile, tile)
            normed = (hidb[rows, cols] - mean) * scale * gain_ref[cols][None, :]
            nb[pl.ds(pl.multiple_of(row + EDGE, EDGE), CHUNK), cols] = normed.astype(BF16)
        nrm_copy(c).start()

    project(jnp.int32(1))

    @pl.when(has_right)
    def _():
        for copy in to_right:
            copy.wait_send()

    @pl.when(has_left)
    def _():
        for copy in to_left:
            copy.start()

    project(jnp.int32(2))
    normalise(jnp.int32(1))

    @pl.when(has_left)
    def _():
        for copy in to_right:
            copy.wait_recv()
        turn(0, 0)

    attend(jnp.int32(0))
    normalise(jnp.int32(2))
    project(jnp.int32(0))
    normalise(jnp.int32(0))

    @pl.when(has_left)
    def _():
        edge_left.start()

    tail_rows = frames - EARLY - COARSE * EARLY_SPAN
    early = [EARLY + EARLY_SPAN * r for r in range(COARSE)]
    late = [EARLY + COARSE * EARLY_SPAN + LATE_SPAN * r for r in range(tail_rows // LATE_SPAN)]
    late += [LATE_SPAN * r for r in range(EARLY // LATE_SPAN)]

    def emit(spot, cols, total):
        rows = pl.ds(spot, total.shape[0])
        resb[rows, cols] = (hidb[rows, cols] + silu(total * valid_ref[rows, :])).astype(BF16)

    def both(spots, size, vector):
        def run(i, carry):
            tasks = []
            for half in range(2):
                if half in vector:
                    tasks.append(direct(i * 2 + half, spots, size, wide.at[half], nb, taps_ref, emit))
                else:
                    tasks.append(convolve(
                        i * 2 + half, spots, size, wide.at[half], padded.at[half], rows_of.at[half],
                        shaped.at[half], taps_wide.at[half], sums.at[half], eye_ref, nb, taps_ref, emit,
                    ))
            for _ in range(3):
                for task in tasks:
                    next(task)
            return carry

        return run

    early_step, late_step = both(early, EARLY_SPAN, ()), both(late, LATE_SPAN, (0, 1))
    stops = [sum(FILL[:i]) for i in range(len(FILL) + 1)]

    def fill(i):
        lax.fori_loop(stops[i], stops[i + 1], early_step, 0)

    fill(0)

    @pl.when(has_right)
    def _():
        for copy in to_left:
            copy.wait_recv()
        turn(1 + frames // 128, 0)

    attend(jnp.int32(blocks - 1))
    fill(1)
    project(jnp.int32(chunks - 1))
    fill(2)
    normalise(jnp.int32(chunks - 1))

    @pl.when(has_right)
    def _():
        edge_right.start()

    fill(3)

    @pl.when(has_left)
    def _():
        edge_right.wait_recv()

    @pl.when(jnp.logical_not(has_left))
    def _():
        nb[low_edge] = jnp.zeros((EDGE, feats), BF16)

    @pl.when(has_right)
    def _():
        edge_left.wait_recv()

    @pl.when(jnp.logical_not(has_right))
    def _():
        nb[high_edge] = jnp.zeros((EDGE, feats), BF16)

    edges = (
        pltpu.make_async_copy(nb.at[low_edge], nrm_hbm.at[low_edge], out_sem.at[2 * chunks]),
        pltpu.make_async_copy(nb.at[high_edge], nrm_hbm.at[high_edge], out_sem.at[2 * chunks + 1]),
    )
    for copy in edges:
        copy.start()

    def pre_copy(i):
        cols = pl.ds(pl.multiple_of(i * LANES, LANES), LANES)
        return pltpu.make_async_copy(resb.at[:, cols], pre_hbm.at[:, cols], pre_sem.at[i])

    def finish(i, carry):
        late_step(i, 0)
        pre_copy(i).start()
        return carry

    lax.fori_loop(0, feats // LANES, finish, 0)

    @pl.when(has_right)
    def _():
        edge_right.wait_send()

    @pl.when(has_left)
    def _():
        for copy in (*to_left, edge_left):
            copy.wait_send()

    to_mate.wait_send()

    def drain(c, carry):
        stat_copy(c).wait_send()
        hid_copy(c).wait()
        nrm_copy(c).wait()
        for part in range(CHUNK // BLOCK):
            att_copy(c * (CHUNK // BLOCK) + part).wait_send()
        return carry

    lax.fori_loop(0, chunks, drain, 0)

    def leave(i, carry):
        pre_copy(i).wait()
        return carry

    lax.fori_loop(0, feats // LANES, leave, 0)
    for copy in edges:
        copy.wait()


def on_device(q, k, v, weight, residual, gain, taps, starts, lengths):
    frames, width = q.shape
    feats = residual.shape[1]
    chunks, blocks = frames // CHUNK, frames // BLOCK
    anywhere = pl.BlockSpec(memory_space=pl.ANY)
    scalars = pl.BlockSpec(memory_space=pltpu.SMEM)
    dma = pltpu.SemaphoreType.DMA
    tall = (max(EARLY_SPAN, LATE_SPAN) // PHASES + STEPS - 1) * COARSE
    pre, hidden, normed = pl.pallas_call(
        block_kernel,
        out_shape=(
            jax.ShapeDtypeStruct((frames, feats), BF16),
            jax.ShapeDtypeStruct((frames, feats), F32),
            jax.ShapeDtypeStruct((frames + 2 * EDGE, feats), BF16),
        ),
        in_specs=[scalars, scalars] + [anywhere] * 5 + [pl.BlockSpec(memory_space=pltpu.VMEM)] * 2,
        out_specs=(anywhere,) * 3,
        scratch_shapes=[
            pltpu.VMEM((frames, width), BF16),
            pltpu.VMEM((frames + 2 * WIN, width), BF16),
            pltpu.VMEM((width, frames + 2 * WIN), BF16),
            pltpu.VMEM((frames + 2 * WIN, width), BF16),
            pltpu.VMEM((2, width, feats), BF16),
            pltpu.VMEM((2, frames, width), BF16),
            pltpu.VMEM((frames, feats), BF16),
            pltpu.VMEM((frames, feats), F32),
            pltpu.VMEM((frames + 2 * EDGE, feats), BF16),
            pltpu.VMEM((frames, 128), F32),
            pltpu.VMEM((frames, 128), F32),
            pltpu.VMEM((frames, 128), F32),
            pltpu.VMEM((HALF, 256), BF16),
            pltpu.VMEM((2, COARSE * (EARLY_SPAN + 2 * EDGE + 1), 128), F32),
            pltpu.VMEM((2, 48, 128), F32),
            pltpu.VMEM((2, 2, 40, 256), F32),
            pltpu.VMEM((2, 2, tall, 256), BF16),
            pltpu.VMEM((2, 2, PHASES * STEPS * HALF, 256), BF16),
            pltpu.VMEM((2, COARSE * (EARLY_SPAN + 1), 128), F32),
            dma((5,)), dma((7,)), dma((7,)), dma((blocks,)), dma((blocks,)),
            dma((chunks,)), dma((chunks,)), dma((2 * chunks + 2,)), dma((feats // LANES,)),
        ],
        compiler_params=pltpu.CompilerParams(
            collective_id=0, has_side_effects=True, vmem_limit_bytes=60 * 2**20
        ),
        name="mix",
    )(starts, lengths, q, k, v, weight, residual, gain, taps)
    anchor = (lax.axis_index("seq") * frames).astype(jnp.int32).reshape(1)
    return pl.pallas_call(
        fix_kernel,
        out_shape=jax.ShapeDtypeStruct((frames, feats), BF16),
        in_specs=[scalars] * 3 + [anywhere] * 4,
        out_specs=anywhere,
        scratch_shapes=[
            pltpu.VMEM((frames, feats), BF16),
            pltpu.VMEM((FIX, feats), F32),
            pltpu.VMEM((FIX + 2 * EDGE, feats), BF16),
            pltpu.VMEM((REC, FIX, feats), BF16),
            pltpu.VMEM((KERNEL, feats), F32),
            pltpu.VMEM((FIX + 2 * EDGE, 128), F32),
            pltpu.SMEM((REC,), jnp.int32),
            dma((8,)), dma((3,)),
        ],
        compiler_params=pltpu.CompilerParams(vmem_limit_bytes=60 * 2**20),
        name="fix",
    )(starts, lengths, anchor, pre, hidden, normed, taps)


def solution(mesh):
    placed = (
        P(("grp", "seq"), "tp"),
        P(("grp", "seq"), "tp"),
        P(("grp", "seq"), "tp"),
        P("tp", None),
        P(("grp", "seq"), "tp"),
        P("tp"),
        P(None, "tp"),
        P("grp"),
        P("grp"),
    )
    return jax.shard_map(
        on_device, mesh=mesh, in_specs=placed, out_specs=P(("grp", "seq"), "tp"), check_vma=False
    )
```
